128 devices in a mesh: dp: 8 (over y, x_lo), ctx: 16 (over z, x_hi, core).
Axes of the slice: x: 4 (x_hi: 2, x_lo: 2; x = x_hi * 2 + x_lo), y: 4, z: 4, core: 2. Of those that a mesh axis runs over, the one named last changes fastest.
Arguments:
- queries: bfloat16 [24576, 4096], P(('dp', 'ctx')), may hold values from -6.5 to 6.5
- keys: bfloat16 [24576, 512], P(('dp', 'ctx')), may hold values from -4 to 4
- values: bfloat16 [24576, 512], P(('dp', 'ctx')), may hold values from -6 to 6
- out_grad: bfloat16 [24576, 4096], P(('dp', 'ctx')), may hold values from -6 to 6
- hidden: bfloat16 [24576, 8192], P(('dp', 'ctx')), may hold values from -24 to 24
Outputs:
- query_grad: bfloat16 [24576, 4096], P(('dp', 'ctx'))
- key_grad: bfloat16 [24576, 512], P(('dp', 'ctx'))
- value_grad: bfloat16 [24576, 512], P(('dp', 'ctx'))
- key_weight_grad: float32 [8192, 512], P(('dp', 'ctx'))
- value_weight_grad: float32 [8192, 512], P(('dp', 'ctx'))
The draws below stay inside these ranges and needn't reach their ends.
All inputs are finite; a program needn't handle non-finite values.
Results may differ from the reference program's by a relative error of at most 0.02.
Values may be sent and summed in bfloat16 or wider, within the bound.
A program may use at most 256 MiB of HBM per device.

```python
import math
import jax
import jax.numpy as jnp
from jax import lax

D = 8192
QH = 32
KVH = 4
HD = 128
SEQ = 3072
TOKENS = 24576
QPD = 2
REPL = 4
N_DP = 8


def draw_queries(key, part):
    shape = (TOKENS, QH * HD)
    base = jnp.clip(jax.random.normal(jax.random.fold_in(key, 1), shape, jnp.float32), -4.0, 4.0)
    return base.astype(jnp.bfloat16)


def draw_keys(key, part):
    shape = (TOKENS, KVH * HD)
    base = jnp.clip(jax.random.normal(jax.random.fold_in(key, 2), shape, jnp.float32), -4.0, 4.0)
    return base.astype(jnp.bfloat16)


def spiked(drawn, own_key, source, target, parts, factor):
    def block_of(dim):
        return (jnp.arange(drawn.shape[dim]) // (drawn.shape[dim] // parts)).reshape((-1,) + (1,) * (drawn.ndim - 1 - dim))

    first = jax.random.permutation(own_key, parts)[block_of(target)]
    second = (block_of(target) + parts // 2) % parts
    return jnp.where((block_of(source) == first) | (block_of(source) == second), factor * drawn, drawn)


def block_levels(rng, extent, shards, low, largest):
    factor_of, own = 1.0, jax.random.fold_in(rng, 6)
    for axis_at, blocks in shards:
        draws = jnp.exp(jax.random.uniform(jax.random.fold_in(own, axis_at), (blocks,), jnp.float32, low / len(shards), largest / len(shards)))
        factor_of = factor_of * jnp.repeat(draws, extent[axis_at] // blocks).reshape([-1 if axis == axis_at else 1 for axis in range(len(extent))])
    return factor_of


def scatter_about(rng, dims, deviation, most, pieces=(), kind=jnp.bfloat16):
    values = deviation * jax.random.normal(rng, dims, jnp.float32)
    if pieces:
        values = values * block_levels(rng, dims, pieces, -0.22, 0.18)
    return jnp.clip(values, -most, most).astype(kind)


def bell_draw_with(rng, shape, spread, reach, shards, heavy, held_as=jnp.bfloat16):
    drawn = spread * jax.random.normal(rng, shape, jnp.float32)
    if shards:
        drawn = drawn * block_levels(rng, shape, shards, -0.22, 0.18)
    return jnp.clip(spiked(drawn, jax.random.fold_in(rng, 3), *heavy), -reach, reach).astype(held_as)


def setup_inputs(seed: int = 0) -> dict:
    splits = jax.random.split(jax.random.key(seed), 6)
    queries = draw_queries(jax.random.fold_in(splits[5], 71), 0)
    keys = draw_keys(jax.random.fold_in(splits[5], 71), 0)
    values = scatter_about(splits[2], (TOKENS, KVH * HD), 1.0, 6.0, ((0, 128),))
    out_grad = scatter_about(splits[3], (TOKENS, QH * HD), 1.0, 6.0, ((0, 128),))
    hidden = bell_draw_with(splits[4], (TOKENS, D), 1.0, 24.0, ((0, 128),), (0, 1, 128, 5.5))
    return {"queries": queries, "keys": keys, "values": values, "out_grad": out_grad, "hidden": hidden}


def head_backward(inputs):
    query, key_row, value_row, grad_out = inputs
    score_scale = 1.0 / math.sqrt(HD)
    scores = jnp.dot(query, key_row.T, preferred_element_type=jnp.float32) * score_scale
    row_ids = lax.broadcasted_iota(jnp.int32, scores.shape, 0)
    col_ids = lax.broadcasted_iota(jnp.int32, scores.shape, 1)
    scores = jnp.where(col_ids <= row_ids, scores, -jnp.inf)
    row_max = lax.optimization_barrier(jnp.max(scores, axis=1, keepdims=True))
    exponent = jnp.exp(scores - row_max)
    probability = exponent / lax.optimization_barrier(jnp.sum(exponent, axis=1, keepdims=True))
    prob_low = probability.astype(jnp.bfloat16)
    attended = jnp.dot(prob_low, value_row, preferred_element_type=jnp.float32)
    row_delta = lax.optimization_barrier(jnp.sum(grad_out.astype(jnp.float32) * attended, axis=1, keepdims=True))
    prob_grad = jnp.dot(grad_out, value_row.T, preferred_element_type=jnp.float32)
    score_grad = (probability * (prob_grad - row_delta)).astype(jnp.bfloat16)
    query_grad = (jnp.dot(score_grad, key_row, preferred_element_type=jnp.float32) * score_scale).astype(jnp.bfloat16)
    key_grad = jnp.dot(score_grad.T, query, preferred_element_type=jnp.float32) * score_scale
    value_grad = jnp.dot(prob_low.T, grad_out, preferred_element_type=jnp.float32)
    return (query_grad, key_grad, value_grad)

def combine_heads(per_head):
    partial_value = lax.optimization_barrier(jnp.sum(per_head.reshape(KVH, REPL, QPD, SEQ, HD), axis=2)).astype(jnp.bfloat16)
    total = lax.optimization_barrier(jnp.sum(partial_value.astype(jnp.float32), axis=1)).astype(jnp.bfloat16)
    return total.transpose(1, 0, 2).reshape(SEQ, KVH * HD)

def sequence_backward(inputs):
    query_seq, key_seq, value_seq, grad_seq = inputs
    group = QH // KVH
    query_heads = query_seq.reshape(SEQ, QH, HD).transpose(1, 0, 2)
    grad_heads = grad_seq.reshape(SEQ, QH, HD).transpose(1, 0, 2)
    key_heads = jnp.repeat(key_seq.reshape(SEQ, KVH, HD).transpose(1, 0, 2), group, axis=0)
    value_heads = jnp.repeat(value_seq.reshape(SEQ, KVH, HD).transpose(1, 0, 2), group, axis=0)
    query_grad, key_grad, value_grad = lax.map(head_backward, (query_heads, key_heads, value_heads, grad_heads))
    query_grad = query_grad.transpose(1, 0, 2).reshape(SEQ, QH * HD)
    return (query_grad, combine_heads(key_grad), combine_heads(value_grad))

def reference(queries, keys, values, out_grad, hidden):
    query_grad, key_grad, value_grad = lax.map(sequence_backward, (queries.reshape(N_DP, SEQ, QH * HD), keys.reshape(N_DP, SEQ, KVH * HD), values.reshape(N_DP, SEQ, KVH * HD), out_grad.reshape(N_DP, SEQ, QH * HD)))
    query_grad = query_grad.reshape(TOKENS, QH * HD)
    key_grad = key_grad.reshape(TOKENS, KVH * HD)
    value_grad = value_grad.reshape(TOKENS, KVH * HD)
    contract = (((0,), (0,)), ((), ()))
    key_weight_grad = lax.dot_general(hidden, key_grad, contract, preferred_element_type=jnp.float32)
    value_weight_grad = lax.dot_general(hidden, value_grad, contract, preferred_element_type=jnp.float32)
    return (query_grad, key_grad, value_grad, key_weight_grad, value_weight_grad)
```

```python
import functools
import math

import jax
import jax.numpy as jnp
from jax import lax
from jax.experimental import pallas as pl
from jax.experimental.pallas import tpu as pltpu
from jax.sharding import PartitionSpec as P

MESH = pl.DeviceIdType.MESH
HD = 128
NZ, NX, NC = 4, 2, 2
NB = NZ * NX
LANES = 768
SCALE = 1.0 / math.sqrt(HD)
SCALE2 = SCALE * math.log2(math.e)
F32, BF16 = jnp.float32, jnp.bfloat16


def dot(a, b, ca=1, cb=0):
    return lax.dot_general(a, b, (((ca,), (cb,)), ((), ())), preferred_element_type=F32)


def kernel(
    n_dp,
    q_in,
    k_in,
    v_in,
    g_in,
    h_in,
    dq_out,
    dk_out,
    dv_out,
    wk_out,
    wv_out,
    q_buf,
    g_buf,
    kv_buf,
    q_t,
    g_t,
    e_buf,
    p_buf,
    m_buf,
    acc,
    dq_buf,
    core_send,
    core_recv,
    x_send,
    x_recv,
    fin,
    h_buf,
    kvg,
    w_part,
    wc_send,
    wc_recv,
    w_send,
    w_recv,
    w_k,
    w_v,
    s_q,
    s_g,
    s_kv,
    s_fw,
    s_h,
    s_dq,
    s_misc,
    r_q,
    r_g,
    r_kv,
    r_fw,
    r_h,
    r_dq,
    r_core,
    r_x,
    r_fin,
    r_kvg,
    r_wc,
    r_w,
    o_sem,
):
    me_dp = lax.axis_index("dp")
    me = lax.axis_index("ctx")
    z, x, c = me // (NX * NC), (me // NC) % NX, me % NC
    oc = 1 - c
    tok = q_in.shape[0]
    blk = tok * NC
    heads = q_in.shape[1] // HD
    per_dev = heads // (NZ * NC)
    kv_cols = k_in.shape[1]
    rows = per_dev * blk

    def ctx_dev(zz, xx, cc):
        return (me_dp, (zz * NX + xx) * NC + cc)

    def remote(src, dst, ssem, rsem, dev):
        return pltpu.make_async_remote_copy(
            src_ref=src, dst_ref=dst, send_sem=ssem, recv_sem=rsem, device_id=dev, device_id_type=MESH
        )

    def wait_bytes(ref, sem):
        pltpu.make_async_copy(ref, ref, sem).wait()

    barrier = pltpu.get_barrier_semaphore()
    n_ctx = NZ * NX * NC
    for d in range(1, n_ctx):
        pl.semaphore_signal(barrier, inc=1, device_id=(me_dp, lax.rem(me + d, n_ctx)), device_id_type=MESH)
    for d in range(1, n_dp):
        pl.semaphore_signal(barrier, inc=1, device_id=(lax.rem(me_dp + d, n_dp), me), device_id_type=MESH)
    pl.semaphore_wait(barrier, n_ctx - 1 + n_dp - 1)

    my_block = z * NX + x
    for dz in range(NZ):
        gz = lax.rem(z + dz, NZ)
        cols = pl.ds(pl.multiple_of(gz * HD, HD), HD)
        for dx in range(NX):
            gx = lax.rem(x + dx, NX)
            for which, src in ((0, k_in), (1, v_in)):
                dst = kv_buf.at[my_block, c, which]
                if dz == 0 and dx == 0:
                    pltpu.make_async_copy(src.at[:, cols], dst, r_kv.at[my_block]).start()
                else:
                    remote(src.at[:, cols], dst, s_kv, r_kv.at[my_block], ctx_dev(gz, gx, c)).start()
    for dz in range(NZ):
        gz = lax.rem(z + dz, NZ)
        for dc in range(NC):
            gc = lax.rem(c + dc, NC)
            for a in range(per_dev):
                col = ((gz * NC + gc) * per_dev + a) * HD
                cols = pl.ds(pl.multiple_of(col, HD), HD)
                spot = pl.ds(pl.multiple_of(c * tok, tok), tok)
                for src, buf, ssem, rsem in ((q_in, q_buf, s_q, r_q), (g_in, g_buf, s_g, r_g)):
                    dst = buf.at[z, a, spot, :]
                    if dz == 0 and dc == 0:
                        pltpu.make_async_copy(src.at[:, cols], dst, rsem.at[z]).start()
                    else:
                        remote(src.at[:, cols], dst, ssem, rsem.at[z], ctx_dev(gz, x, gc)).start()
    share = h_in.shape[1] // n_dp
    for d in range(n_dp):
        gd = lax.rem(me_dp + d, n_dp)
        cols = pl.ds(pl.multiple_of(gd * share, HD), share)
        if d == 0:
            pltpu.make_async_copy(h_in.at[:, cols], h_buf.at[me_dp], r_h).start()
        else:
            remote(h_in.at[:, cols], h_buf.at[me_dp], s_h, r_h, (gd, me)).start()

    acc[...] = jnp.zeros_like(acc)
    for d in range(NB):
        b = lax.rem(my_block + d, NB)
        wait_bytes(kv_buf.at[b, c], r_kv.at[b])
        remote(kv_buf.at[b, c], kv_buf.at[b, c], s_fw.at[b], r_fw.at[b], ctx_dev(z, x, oc)).start()
    for d in range(NB):
        b = lax.rem(my_block + d, NB)
        wait_bytes(kv_buf.at[b, oc], r_fw.at[b])

    def attend(step, carry):
        later = NZ - step
        zq = jnp.where(step == 0, z, jnp.where(later <= z, later - 1, later))
        last = zq * NX + x
        wait_bytes(q_buf.at[zq], r_q.at[zq])
        wait_bytes(g_buf.at[zq], r_g.at[zq])
        for a in range(per_dev):
            q_t[:, a * blk : (a + 1) * blk] = q_buf[zq, a].T
            g_t[:, a * blk : (a + 1) * blk] = g_buf[zq, a].T
        heads_in = LANES // blk
        for part in range(rows // LANES):
            lanes = slice(part * LANES, (part + 1) * LANES)
            qt, gt = q_t[:, lanes], g_t[:, lanes]
            hs = pl.ds(part * heads_in, heads_in)

            def first(b, carry, masked):
                top, total, delta = carry
                at = pl.ds(pl.multiple_of(b * blk, blk), blk)
                kb = kv_buf[b, :, 0].reshape(blk, HD)
                vb = kv_buf[b, :, 1].reshape(blk, HD)
                s = dot(kb, qt) * SCALE2
                if masked:
                    key_id = lax.broadcasted_iota(jnp.int32, (blk, blk), 0)
                    query_id = lax.broadcasted_iota(jnp.int32, (blk, blk), 1)
                    seen = key_id <= query_id
                    s = jnp.concatenate(
                        [jnp.where(seen, s[:, i * blk : (i + 1) * blk], -jnp.inf) for i in range(heads_in)], 1
                    )
                dp = dot(vb, gt)
                new = jnp.maximum(top, jnp.max(s, axis=0, keepdims=True))
                shrink = jnp.exp2(top - new)
                e = jnp.exp2(s - new)
                total = total * shrink + jnp.sum(e, axis=0, keepdims=True)
                delta = delta * shrink + jnp.sum(e * dp, axis=0, keepdims=True)
                e_buf[at, :] = e
                p_buf[at, :] = dp
                m_buf[pl.ds(b, 1), :] = new
                return new, total, delta

            zero = jnp.zeros((1, LANES), F32)
            stats = lax.fori_loop(0, last, lambda b, t: first(b, t, False), (zero - jnp.inf, zero, zero))
            top, total, delta = first(last, stats, True)
            inv = 1.0 / total
            delta = delta * inv

            def second(b, dqt):
                at = pl.ds(pl.multiple_of(b * blk, blk), blk)
                fix = jnp.exp2(m_buf[pl.ds(b, 1), :] - top) * inv
                prob = e_buf[at, :] * fix
                low = prob.astype(BF16)
                ds = (prob * (p_buf[at, :] - delta)).astype(BF16)
                kb = kv_buf[b, :, 0].reshape(blk, HD)
                gh = g_buf[zq, hs].reshape(LANES, HD)
                qh = q_buf[zq, hs].reshape(LANES, HD)
                acc[0, b] += dot(ds, qh).reshape(NC, tok, HD)
                acc[1, b] += dot(low, gh).reshape(NC, tok, HD)
                return dqt + dot(kb.T, ds)

            dqt = lax.fori_loop(0, last + 1, second, jnp.zeros((HD, LANES), F32))
            for i in range(heads_in):
                head = dqt[:, i * blk : (i + 1) * blk] * SCALE
                dq_buf[zq, part * heads_in + i] = head.T.astype(BF16)
        for gc in range(NC):
            mine = jnp.logical_and(zq == z, c == gc)
            for a in range(per_dev):
                col = ((z * NC + c) * per_dev + a) * HD
                cols = pl.ds(pl.multiple_of(col, HD), HD)
                src = dq_buf.at[zq, a, gc * tok : (gc + 1) * tok, :]

                @pl.when(mine)
                def _():
                    pltpu.make_async_copy(src, dq_out.at[:, cols], r_dq).start()

                @pl.when(jnp.logical_not(mine))
                def _():
                    remote(src, dq_out.at[:, cols], s_dq, r_dq, ctx_dev(zq, x, gc)).start()

        return carry

    lax.fori_loop(0, NZ, attend, 0)

    for b in range(NB):
        core_send[b, 0] = (acc[0, b, oc] * SCALE).astype(BF16)
        core_send[b, 1] = acc[1, b, oc].astype(BF16)
    over_core = remote(core_send, core_recv, s_misc.at[0], r_core, ctx_dev(z, x, oc))
    over_core.start()
    over_core.wait()
    for zz in range(NZ):
        b = zz * NX + (1 - x)
        x_send[zz, 0] = (acc[0, b, c] * SCALE + core_recv[b, 0].astype(F32)).astype(BF16)
        x_send[zz, 1] = (acc[1, b, c] + core_recv[b, 1].astype(F32)).astype(BF16)
    over_x = remote(x_send, x_recv, s_misc.at[1], r_x, ctx_dev(z, 1 - x, c))
    over_x.start()
    over_x.wait()
    for zz in range(NZ):
        b = zz * NX + x
        fin[zz, 0] = (
            acc[0, b, c] * SCALE + core_recv[b, 0].astype(F32) + x_recv[zz, 0].astype(F32)
        ).astype(BF16)
        fin[zz, 1] = (acc[1, b, c] + core_recv[b, 1].astype(F32) + x_recv[zz, 1].astype(F32)).astype(BF16)
    for dz in range(NZ):
        gz = lax.rem(z + dz, NZ)
        for which in range(2):
            cols = pl.ds(pl.multiple_of(which * kv_cols + z * HD, HD), HD)
            dst = kvg.at[me_dp, :, cols]
            if dz == 0:
                pltpu.make_async_copy(fin.at[gz, which], dst, r_fin).start()
            else:
                remote(fin.at[gz, which], dst, s_misc.at[2], r_fin, ctx_dev(gz, x, c)).start()
    wait_bytes(kvg.at[me_dp], r_fin)
    for d in range(1, n_dp):
        gd = lax.rem(me_dp + d, n_dp)
        remote(kvg.at[me_dp], kvg.at[me_dp], s_misc.at[3], r_kvg.at[me_dp], (gd, me)).start()
    out_k = pltpu.make_async_copy(kvg.at[me_dp, :, 0:kv_cols], dk_out, o_sem.at[0])
    out_v = pltpu.make_async_copy(kvg.at[me_dp, :, kv_cols : 2 * kv_cols], dv_out, o_sem.at[1])
    out_k.start()
    out_v.start()
    wait_bytes(h_buf, r_h)
    for d in range(1, n_dp):
        gd = lax.rem(me_dp + d, n_dp)
        wait_bytes(kvg.at[gd], r_kvg.at[gd])
    width = 2 * kv_cols
    grads = kvg[...].reshape(n_dp * tok, width)
    out_rows = w_part.shape[2]
    chunk = NX * NC * out_rows

    def project(zz, carry):
        cols = pl.ds(pl.multiple_of(zz * chunk, chunk), chunk)
        hid = h_buf[:, :, cols].reshape(n_dp * tok, chunk)
        res = dot(hid, grads, 0, 0)
        w_part[pl.ds(zz * NX, NX)] = res.reshape(NX, NC, out_rows, width)
        return carry

    lax.fori_loop(0, NZ, project, 0)
    for b in range(NB):
        wc_send[b] = w_part[b, oc].astype(BF16)
    over_core = remote(wc_send, wc_recv, s_misc.at[4], r_wc, ctx_dev(z, x, oc))
    over_core.start()
    over_core.wait()
    for b in range(NB):
        w_send[b] = (w_part[b, c] + wc_recv[b].astype(F32)).astype(BF16)
    for d in range(1, NB):
        b = lax.rem(my_block + d, NB)
        remote(
            w_send.at[b], w_recv.at[my_block], s_misc.at[5], r_w.at[my_block], ctx_dev(b // NX, lax.rem(b, NX), c)
        ).start()
    total = w_part[my_block, c] + wc_recv[my_block].astype(F32)
    for d in range(1, NB):
        b = lax.rem(my_block + d, NB)
        wait_bytes(w_recv.at[b], r_w.at[b])
        total = total + w_recv[b].astype(F32)
    w_k[...] = total[:, :kv_cols]
    w_v[...] = total[:, kv_cols:]
    out_wk = pltpu.make_async_copy(w_k, wk_out, o_sem.at[2])
    out_wv = pltpu.make_async_copy(w_v, wv_out, o_sem.at[3])
    out_wk.start()
    out_wv.start()

    wait_bytes(dq_out, r_dq)
    part = heads - per_dev
    wait_bytes(q_in.at[:, : part * HD], s_q)
    wait_bytes(g_in.at[:, : part * HD], s_g)
    wait_bytes(q_in.at[:, : part * HD], s_dq)
    wait_bytes(q_in.at[:, : (NB - 1) * 2 * HD], s_kv)
    for b in range(NB):
        wait_bytes(kv_buf.at[b, c], s_fw.at[b])
    wait_bytes(h_in.at[:, : (n_dp - 1) * share], s_h)
    wait_bytes(fin.at[pl.ds(0, NZ - 1)], s_misc.at[2])
    wait_bytes(kvg.at[pl.ds(0, n_dp - 1)], s_misc.at[3])
    wait_bytes(w_send.at[pl.ds(0, NB - 1)], s_misc.at[5])
    out_k.wait()
    out_v.wait()
    out_wk.wait()
    out_wv.wait()


def on_device(n_dp, queries, keys, values, out_grad, hidden):
    tok, width = queries.shape
    kv_cols = keys.shape[1]
    blk = tok * NC
    per_dev = width // HD // (NZ * NC)
    rows = per_dev * blk
    share = hidden.shape[1] // n_dp
    out_rows = share // (NZ * NX * NC)
    dma = pltpu.SemaphoreType.DMA
    any_spec = pl.BlockSpec(memory_space=pl.ANY)
    return pl.pallas_call(
        functools.partial(kernel, n_dp),
        out_shape=[
            jax.ShapeDtypeStruct(queries.shape, BF16),
            jax.ShapeDtypeStruct(keys.shape, BF16),
            jax.ShapeDtypeStruct(values.shape, BF16),
            jax.ShapeDtypeStruct((out_rows, kv_cols), F32),
            jax.ShapeDtypeStruct((out_rows, kv_cols), F32),
        ],
        in_specs=[any_spec] * 5,
        out_specs=[any_spec] * 5,
        scratch_shapes=[
            pltpu.VMEM((NZ, per_dev, blk, HD), BF16),
            pltpu.VMEM((NZ, per_dev, blk, HD), BF16),
            pltpu.VMEM((NB, NC, 2, tok, HD), BF16),
            pltpu.VMEM((HD, rows), BF16),
            pltpu.VMEM((HD, rows), BF16),
            pltpu.VMEM((NB * blk, LANES), F32),
            pltpu.VMEM((NB * blk, LANES), F32),
            pltpu.VMEM((NB, LANES), F32),
            pltpu.VMEM((2, NB, NC, tok, HD), F32),
            pltpu.VMEM((NZ, per_dev, blk, HD), BF16),
            pltpu.VMEM((NB, 2, tok, HD), BF16),
            pltpu.VMEM((NB, 2, tok, HD), BF16),
            pltpu.VMEM((NZ, 2, tok, HD), BF16),
            pltpu.VMEM((NZ, 2, tok, HD), BF16),
            pltpu.VMEM((NZ, 2, tok, HD), BF16),
            pltpu.VMEM((n_dp, tok, share), BF16),
            pltpu.VMEM((n_dp, tok, 2 * kv_cols), BF16),
            pltpu.VMEM((NB, NC, out_rows, 2 * kv_cols), F32),
            pltpu.VMEM((NB, out_rows, 2 * kv_cols), BF16),
            pltpu.VMEM((NB, out_rows, 2 * kv_cols), BF16),
            pltpu.VMEM((NB, out_rows, 2 * kv_cols), BF16),
            pltpu.VMEM((NB, out_rows, 2 * kv_cols), BF16),
            pltpu.VMEM((out_rows, kv_cols), F32),
            pltpu.VMEM((out_rows, kv_cols), F32),
            dma,
            dma,
            dma,
            dma((NB,)),
            dma,
            dma,
            dma((6,)),
            dma((NZ,)),
            dma((NZ,)),
            dma((NB,)),
            dma((NB,)),
            dma,
            dma,
            dma,
            dma,
            dma,
            dma((n_dp,)),
            dma,
            dma((NB,)),
            dma((4,)),
        ],
        compiler_params=pltpu.CompilerParams(
            collective_id=0, has_side_effects=True, vmem_limit_bytes=58 * 1024 * 1024
        ),
        cost_estimate=pl.CostEstimate(
            flops=40_000_000_000, bytes_accessed=20_000_000, transcendentals=10_000_000
        ),
        name="attention_backward",
    )(queries, keys, values, out_grad, hidden)


def solution(mesh):
    spec = P(("dp", "ctx"), None)
    return jax.shard_map(
        functools.partial(on_device, mesh.shape["dp"]),
        mesh=mesh,
        in_specs=(spec,) * 5,
        out_specs=(spec,) * 5,
        check_vma=False,
    )
```

```python
import functools
import math

import jax
import jax.numpy as jnp
from jax import lax
from jax.experimental import pallas as pl
from jax.experimental.pallas import tpu as pltpu
from jax.sharding import PartitionSpec as P

MESH = pl.DeviceIdType.MESH
HD = 128
NZ, NX, NC = 4, 2, 2
NB = NZ * NX
SCALE = 1.0 / math.sqrt(HD)
SCALE2 = SCALE * math.log2(math.e)
F32, BF16 = jnp.float32, jnp.bfloat16


def dot(a, b, ca=1, cb=0):
    return lax.dot_general(a, b, (((ca,), (cb,)), ((), ())), preferred_element_type=F32)


def kernel(
    n_dp,
    q_in,
    k_in,
    v_in,
    g_in,
    h_in,
    dq_out,
    dk_out,
    dv_out,
    wk_out,
    wv_out,
    q_buf,
    g_buf,
    kv_buf,
    q_t,
    g_t,
    e_buf,
    p_buf,
    m_buf,
    acc,
    dq_buf,
    core_send,
    core_recv,
    x_send,
    x_recv,
    fin,
    h_buf,
    kvg,
    wc_send,
    wc_recv,
    w_send,
    w_recv,
    w_res,
    s_q,
    s_g,
    s_kv,
    s_fw,
    s_h,
    s_dq,
    s_core,
    s_x,
    s_fin,
    s_a,
    s_wc,
    s_w,
    r_q,
    r_g,
    r_kv,
    r_fw,
    r_h,
    r_dq,
    r_core,
    r_x,
    r_fin,
    r_a,
    r_wc,
    r_w,
    o_sem,
):
    me_dp = lax.axis_index("dp")
    me = lax.axis_index("ctx")
    z, x, c = me // (NX * NC), (me // NC) % NX, me % NC
    oc = 1 - c
    tok = q_in.shape[0]
    blk = tok * NC
    heads = q_in.shape[1] // HD
    per_dev = heads // (NZ * NC)
    kv_cols = k_in.shape[1]
    rows = per_dev * blk

    def ctx_dev(zz, xx, cc):
        return (me_dp, (zz * NX + xx) * NC + cc)

    def remote(src, dst, ssem, rsem, dev):
        return pltpu.make_async_remote_copy(
            src_ref=src, dst_ref=dst, send_sem=ssem, recv_sem=rsem, device_id=dev, device_id_type=MESH
        )

    def wait_bytes(ref, sem):
        pltpu.make_async_copy(ref, ref, sem).wait()

    barrier = pltpu.get_barrier_semaphore()
    n_ctx = NZ * NX * NC
    for d in range(1, n_ctx):
        pl.semaphore_signal(barrier, inc=1, device_id=(me_dp, lax.rem(me + d, n_ctx)), device_id_type=MESH)
    for d in range(1, n_dp):
        pl.semaphore_signal(barrier, inc=1, device_id=(lax.rem(me_dp + d, n_dp), me), device_id_type=MESH)
    pl.semaphore_wait(barrier, n_ctx - 1 + n_dp - 1)

    my_block = z * NX + x
    share = h_in.shape[1] // n_dp

    for dz in range(NZ):
        gz = lax.rem(z + dz, NZ)
        cols = pl.ds(pl.multiple_of(gz * HD, HD), HD)
        for dx in range(NX):
            gx = lax.rem(x + dx, NX)
            for which, src in ((0, k_in), (1, v_in)):
                dst = kv_buf.at[my_block, c, which]
                if dz == 0 and dx == 0:
                    pltpu.make_async_copy(src.at[:, cols], dst, r_kv.at[my_block]).start()
                else:
                    remote(src.at[:, cols], dst, s_kv, r_kv.at[my_block], ctx_dev(gz, gx, c)).start()

    def send_queries(dz):
        gz = lax.rem(z + dz, NZ)
        for dc in range(NC):
            gc = lax.rem(c + dc, NC)
            for a in range(per_dev):
                col = ((gz * NC + gc) * per_dev + a) * HD
                cols = pl.ds(pl.multiple_of(col, HD), HD)
                spot = pl.ds(pl.multiple_of(c * tok, tok), tok)
                for src, buf, ssem, rsem in ((q_in, q_buf, s_q, r_q), (g_in, g_buf, s_g, r_g)):
                    dst = buf.at[z, a, spot, :]
                    if dz == 0 and dc == 0:
                        pltpu.make_async_copy(src.at[:, cols], dst, rsem.at[z]).start()
                    else:
                        remote(src.at[:, cols], dst, ssem, rsem.at[z], ctx_dev(gz, x, gc)).start()

    def send_far_queries():
        for dz in range(1, NZ):
            send_queries(dz)

    def send_hidden():
        for d in range(n_dp):
            gd = lax.rem(me_dp + d, n_dp)
            cols = pl.ds(pl.multiple_of(gd * share, HD), share)
            if d == 0:
                pltpu.make_async_copy(h_in.at[:, cols], h_buf.at[me_dp], r_h).start()
            else:
                remote(h_in.at[:, cols], h_buf.at[me_dp], s_h, r_h, (gd, me)).start()

    send_queries(0)
    acc[...] = jnp.zeros_like(acc)
    for d in range(NB):
        b = lax.rem(my_block + d, NB)
        wait_bytes(kv_buf.at[b, c], r_kv.at[b])
        remote(kv_buf.at[b, c], kv_buf.at[b, c], s_fw.at[b], r_fw.at[b], ctx_dev(z, x, oc)).start()
    pl.when(z >= NZ // 2)(send_far_queries)
    for d in range(NB):
        b = lax.rem(my_block + d, NB)
        wait_bytes(kv_buf.at[b, oc], r_fw.at[b])

    def over_core(zz):
        both = pl.ds(zz * NX, NX)
        return remote(core_send.at[both], core_recv.at[both], s_core.at[zz], r_core.at[zz], ctx_dev(z, x, oc))

    def over_x(zz):
        return remote(x_send.at[zz], x_recv.at[zz], s_x.at[zz], r_x.at[zz], ctx_dev(z, 1 - x, c))

    def start_core(zz):
        for b in range(zz * NX, zz * NX + NX):
            core_send[b, 0] = (acc[0, b, oc] * SCALE).astype(BF16)
            core_send[b, 1] = acc[1, b, oc].astype(BF16)
        over_core(zz).start()

    def start_x(zz):
        over_core(zz).wait_recv()
        b = zz * NX + (1 - x)
        x_send[zz, 0] = (acc[0, b, c] * SCALE + core_recv[b, 0].astype(F32)).astype(BF16)
        x_send[zz, 1] = (acc[1, b, c] + core_recv[b, 1].astype(F32)).astype(BF16)
        over_x(zz).start()

    def finish(zz):
        over_x(zz).wait_recv()
        b = zz * NX + x
        fin[zz, 0] = (
            acc[0, b, c] * SCALE + core_recv[b, 0].astype(F32) + x_recv[zz, 0].astype(F32)
        ).astype(BF16)
        fin[zz, 1] = (acc[1, b, c] + core_recv[b, 1].astype(F32) + x_recv[zz, 1].astype(F32)).astype(BF16)
        for which in range(2):
            src = fin.at[zz, which]
            dst = kvg.at[which, me_dp, :, pl.ds(pl.multiple_of(z * HD, HD), HD)]

            @pl.when(z == zz)
            def _():
                pltpu.make_async_copy(src, dst, r_fin.at[which]).start()

            @pl.when(z != zz)
            def _():
                remote(src, dst, s_fin, r_fin.at[which], ctx_dev(zz, x, c)).start()

    def attend(step, carry):
        later = NZ - step
        zq = jnp.where(step == 0, z, jnp.where(later <= z, later - 1, later))
        last = zq * NX + x
        wait_bytes(q_buf.at[zq], r_q.at[zq])
        wait_bytes(g_buf.at[zq], r_g.at[zq])
        for a in range(per_dev):
            q_t[:, a * blk : (a + 1) * blk] = q_buf[zq, a].T
            g_t[:, a * blk : (a + 1) * blk] = g_buf[zq, a].T
        qt, gt = q_t[...], g_t[...]

        def first(b, carry, masked):
            top, total, delta = carry
            at = pl.ds(pl.multiple_of(b * blk, blk), blk)
            kb = kv_buf[b, :, 0].reshape(blk, HD)
            vb = kv_buf[b, :, 1].reshape(blk, HD)
            s = dot(kb, qt) * SCALE2
            if masked:
                key_id = lax.broadcasted_iota(jnp.int32, (blk, blk), 0)
                query_id = lax.broadcasted_iota(jnp.int32, (blk, blk), 1)
                seen = key_id <= query_id
                s = jnp.concatenate(
                    [jnp.where(seen, s[:, i * blk : (i + 1) * blk], -jnp.inf) for i in range(per_dev)], 1
                )
            dp = dot(vb, gt)
            new = jnp.maximum(top, jnp.max(s, axis=0, keepdims=True))
            shrink = jnp.exp2(top - new)
            e = jnp.exp2(s - new)
            total = total * shrink + jnp.sum(e, axis=0, keepdims=True)
            delta = delta * shrink + jnp.sum(e * dp, axis=0, keepdims=True)
            e_buf[at, :] = e.astype(BF16)
            p_buf[at, :] = dp
            m_buf[pl.ds(b, 1), :] = new
            return new, total, delta

        zero = jnp.zeros((1, rows), F32)
        stats = lax.fori_loop(0, last, lambda b, t: first(b, t, False), (zero - jnp.inf, zero, zero))
        top, total, delta = first(last, stats, True)
        inv = 1.0 / total
        delta = delta * inv

        def second(b, dqt):
            at = pl.ds(pl.multiple_of(b * blk, blk), blk)
            fix = jnp.exp2(m_buf[pl.ds(b, 1), :] - top) * inv
            prob = e_buf[at, :].astype(F32) * fix
            low = prob.astype(BF16)
            ds = (prob * (p_buf[at, :] - delta)).astype(BF16)
            kb = kv_buf[b, :, 0].reshape(blk, HD)
            acc[0, b] += dot(ds, q_buf[zq].reshape(rows, HD)).reshape(NC, tok, HD)
            acc[1, b] += dot(low, g_buf[zq].reshape(rows, HD)).reshape(NC, tok, HD)
            return dqt + dot(kb.T, ds)

        dqt = lax.fori_loop(0, last + 1, second, jnp.zeros((HD, rows), F32))
        for a in range(per_dev):
            dq_buf[zq, a] = (dqt[:, a * blk : (a + 1) * blk] * SCALE).T.astype(BF16)
        for gc in range(NC):
            mine = jnp.logical_and(zq == z, c == gc)
            for a in range(per_dev):
                col = ((z * NC + c) * per_dev + a) * HD
                cols = pl.ds(pl.multiple_of(col, HD), HD)
                src = dq_buf.at[zq, a, gc * tok : (gc + 1) * tok, :]

                @pl.when(mine)
                def _():
                    pltpu.make_async_copy(src, dq_out.at[:, cols], r_dq).start()

                @pl.when(jnp.logical_not(mine))
                def _():
                    remote(src, dq_out.at[:, cols], s_dq, r_dq, ctx_dev(zq, x, gc)).start()

        pl.when(jnp.logical_and(step == 0, z < NZ // 2))(send_far_queries)

        @pl.when(step == 1)
        def _():
            start_core(NZ - 1)
            send_hidden()

        @pl.when(step == 2)
        def _():
            start_core(NZ - 2)
            start_x(NZ - 1)

        return carry

    lax.fori_loop(0, NZ, attend, 0)
    start_core(0)
    start_core(1)
    start_x(2)
    start_x(0)
    start_x(1)
    for zz in range(NZ - 1, -1, -1):
        finish(zz)

    half = tok // 2
    y, xl = me_dp // 2, me_dp % 2
    n_y = n_dp // 2
    up_y, down_y, far_y = lax.rem(y + 1, n_y), lax.rem(y + n_y - 1, n_y), lax.rem(y + 2, n_y)
    partner, up, down = y * 2 + (1 - xl), up_y * 2 + xl, down_y * 2 + xl
    up_p, down_p = up_y * 2 + (1 - xl), down_y * 2 + (1 - xl)
    low_half, high_half = pl.ds(0, half), pl.ds(half, half)
    every = pl.ds(0, tok)

    def pass_on(h, source, part, to, n):
        spot = kvg.at[h, source, part, :]
        return remote(spot, spot, s_a.at[h, n], r_a.at[h, n], (to, me))

    def hop(h, n):
        return (
            lambda: pass_on(h, me_dp, every, partner, 0),
            lambda: pass_on(h, me_dp, every, up, 1),
            lambda: pass_on(h, me_dp, every, down, 2),
            lambda: pass_on(h, partner, every, up, 3),
            lambda: pass_on(h, partner, every, down, 4),
            lambda: pass_on(h, down, low_half, up, 5),
            lambda: pass_on(h, up, high_half, down, 6),
            lambda: pass_on(h, down_p, low_half, up, 7),
            lambda: pass_on(h, up_p, high_half, down, 8),
        )[n]()

    def arrived(h, n):
        far, far_p = far_y * 2 + xl, far_y * 2 + (1 - xl)
        source, part = (
            (partner, every),
            (down, every),
            (up, every),
            (down_p, every),
            (up_p, every),
            (far, low_half),
            (far, high_half),
            (far_p, low_half),
            (far_p, high_half),
        )[n]
        wait_bytes(kvg.at[h, source, part, :], r_a.at[h, n])

    def own(h):
        wait_bytes(kvg.at[h, me_dp], r_fin.at[h])
        for n in range(3):
            hop(h, n).start()
        out = pltpu.make_async_copy(kvg.at[h, me_dp], (dk_out, dv_out)[h], o_sem.at[h])
        out.start()

    def relay(h, n, sends):
        arrived(h, n)
        for m in sends:
            hop(h, m).start()

    out_rows = share // (NB * NC)
    n_tok = n_dp * tok

    def project(h):
        cols = slice(h * kv_cols, (h + 1) * kv_cols)
        grads = kvg[h].reshape(n_tok, kv_cols)
        step_rows = share // NZ
        for i in range(NZ):
            at = slice(i * step_rows, (i + 1) * step_rows)
            p_buf[at, cols] = dot(e_buf[at, 0:n_tok], grads)
        for b in range(NB):
            at = pl.ds(pl.multiple_of((b * NC + oc) * out_rows, out_rows), out_rows)
            wc_send[h, b] = p_buf[at, cols].astype(BF16)
        w_core(h).start()

    def w_core(h):
        return remote(wc_send.at[h], wc_recv.at[h], s_wc.at[h], r_wc.at[h], ctx_dev(z, x, oc))

    def partial_sum(h, b):
        at = pl.ds(pl.multiple_of((b * NC + c) * out_rows, out_rows), out_rows)
        return p_buf[at, h * kv_cols : (h + 1) * kv_cols] + wc_recv[h, b].astype(F32)

    def spread(h):
        w_core(h).wait_recv()
        for d in range(1, NB):
            b = lax.rem(my_block + d, NB)
            w_send[h, b] = partial_sum(h, b).astype(BF16)
            dev = ctx_dev(b // NX, lax.rem(b, NX), c)
            remote(w_send.at[h, b], w_recv.at[h, my_block], s_w.at[h], r_w.at[h, my_block], dev).start()

    def collect(h):
        total = partial_sum(h, my_block)
        for d in range(1, NB):
            b = lax.rem(my_block + d, NB)
            wait_bytes(w_recv.at[h, b], r_w.at[h, b])
            total = total + w_recv[h, b].astype(F32)
        w_res[h] = total
        pltpu.make_async_copy(w_res.at[h], (wk_out, wv_out)[h], o_sem.at[2 + h]).start()

    own(0)
    wait_bytes(h_buf, r_h)
    for d in range(0, n_dp, 2):
        e_buf[0:share, d * tok : (d + 2) * tok] = h_buf[d : d + 2].reshape(2 * tok, share).T
    relay(0, 0, (3, 4))
    own(1)
    relay(0, 1, (5,))
    relay(0, 2, (6,))
    relay(1, 0, (3, 4))
    relay(0, 3, (7,))
    relay(0, 4, (8,))
    relay(1, 1, (5,))
    relay(1, 2, (6,))
    for n in range(5, 9):
        arrived(0, n)
    project(0)
    relay(1, 3, (7,))
    relay(1, 4, (8,))
    spread(0)
    for n in range(5, 9):
        arrived(1, n)
    project(1)
    spread(1)
    collect(0)
    collect(1)

    wait_bytes(dq_out, r_dq)
    part = heads - per_dev
    wait_bytes(q_in.at[:, : part * HD], s_q)
    wait_bytes(g_in.at[:, : part * HD], s_g)
    wait_bytes(q_in.at[:, : part * HD], s_dq)
    wait_bytes(q_in.at[:, : (NB - 1) * 2 * HD], s_kv)
    for b in range(NB):
        wait_bytes(kv_buf.at[b, c], s_fw.at[b])
    wait_bytes(h_in.at[:, : (n_dp - 1) * share], s_h)
    for zz in range(NZ):
        over_core(zz).wait_send()
        over_x(zz).wait_send()
    wait_bytes(fin.at[pl.ds(0, NZ - 1)], s_fin)
    for h in range(2):
        for n in range(9):
            hop(h, n).wait_send()
        w_core(h).wait_send()
        wait_bytes(w_send.at[h, pl.ds(0, NB - 1)], s_w.at[h])
        wait_bytes(kvg.at[h, me_dp], o_sem.at[h])
        wait_bytes(w_res.at[h], o_sem.at[2 + h])


def copy_out(*refs):
    sems = refs[-1]
    n = (len(refs) - 1) // 2
    copies = [pltpu.make_async_copy(refs[i], refs[n + i], sems.at[i]) for i in range(n)]
    for copy in copies:
        copy.start()
    for copy in copies:
        copy.wait()


def on_device(n_dp, queries, keys, values, out_grad, hidden):
    tok, width = queries.shape
    kv_cols = keys.shape[1]
    blk = tok * NC
    per_dev = width // HD // (NZ * NC)
    rows = per_dev * blk
    share = hidden.shape[1] // n_dp
    out_rows = share // (NZ * NX * NC)
    dma = pltpu.SemaphoreType.DMA
    any_spec = pl.BlockSpec(memory_space=pl.ANY)
    assert n_dp * tok <= rows and share <= NB * blk and 2 * kv_cols <= rows and n_dp == 8
    shapes = [
        jax.ShapeDtypeStruct(queries.shape, BF16),
        jax.ShapeDtypeStruct(keys.shape, BF16),
        jax.ShapeDtypeStruct(values.shape, BF16),
        jax.ShapeDtypeStruct((out_rows, kv_cols), F32),
        jax.ShapeDtypeStruct((out_rows, kv_cols), F32),
    ]
    results = pl.pallas_call(
        functools.partial(kernel, n_dp),
        out_shape=shapes,
        in_specs=[any_spec] * 5,
        out_specs=[any_spec] * 5,
        scratch_shapes=[
            pltpu.VMEM((NZ, per_dev, blk, HD), BF16),
            pltpu.VMEM((NZ, per_dev, blk, HD), BF16),
            pltpu.VMEM((NB, NC, 2, tok, HD), BF16),
            pltpu.VMEM((HD, rows), BF16),
            pltpu.VMEM((HD, rows), BF16),
            pltpu.VMEM((NB * blk, rows), BF16),
            pltpu.VMEM((NB * blk, rows), F32),
            pltpu.VMEM((NB, rows), F32),
            pltpu.VMEM((2, NB, NC, tok, HD), F32),
            pltpu.VMEM((NZ, per_dev, blk, HD), BF16),
            pltpu.VMEM((NB, 2, tok, HD), BF16),
            pltpu.VMEM((NB, 2, tok, HD), BF16),
            pltpu.VMEM((NZ, 2, tok, HD), BF16),
            pltpu.VMEM((NZ, 2, tok, HD), BF16),
            pltpu.VMEM((NZ, 2, tok, HD), BF16),
            pltpu.VMEM((n_dp, tok, share), BF16),
            pltpu.VMEM((2, n_dp, tok, kv_cols), BF16),
            pltpu.VMEM((2, NB, out_rows, kv_cols), BF16),
            pltpu.VMEM((2, NB, out_rows, kv_cols), BF16),
            pltpu.VMEM((2, NB, out_rows, kv_cols), BF16),
            pltpu.VMEM((2, NB, out_rows, kv_cols), BF16),
            pltpu.VMEM((2, out_rows, kv_cols), F32),
            dma,
            dma,
            dma,
            dma((NB,)),
            dma,
            dma,
            dma((NZ,)),
            dma((NZ,)),
            dma,
            dma((2, 9)),
            dma((2,)),
            dma((2,)),
            dma((NZ,)),
            dma((NZ,)),
            dma((NB,)),
            dma((NB,)),
            dma,
            dma,
            dma((NZ,)),
            dma((NZ,)),
            dma((2,)),
            dma((2, 9)),
            dma((2,)),
            dma((2, NB)),
            dma((4,)),
        ],
        compiler_params=pltpu.CompilerParams(
            collective_id=0, has_side_effects=True, vmem_limit_bytes=60 * 1024 * 1024
        ),
        cost_estimate=pl.CostEstimate(
            flops=40_000_000_000, bytes_accessed=20_000_000, transcendentals=10_000_000
        ),
        name="attention_backward",
    )(queries, keys, values, out_grad, hidden)
    return pl.pallas_call(
        copy_out,
        out_shape=shapes,
        in_specs=[any_spec] * 5,
        out_specs=[any_spec] * 5,
        scratch_shapes=[dma((5,))],
        cost_estimate=pl.CostEstimate(flops=0, bytes_accessed=4_500_000, transcendentals=0),
        name="copy_out",
    )(*results)


def solution(mesh):
    spec = P(("dp", "ctx"), None)
    return jax.shard_map(
        functools.partial(on_device, mesh.shape["dp"]),
        mesh=mesh,
        in_specs=(spec,) * 5,
        out_specs=(spec,) * 5,
        check_vma=False,
    )
```

```python
import functools
import math

import jax
import jax.numpy as jnp
from jax import lax
from jax.experimental import pallas as pl
from jax.experimental.pallas import tpu as pltpu
from jax.sharding import PartitionSpec as P

MESH = pl.DeviceIdType.MESH
HD = 128
NZ, NX, NC = 4, 2, 2
NB = NZ * NX
SCALE = 1.0 / math.sqrt(HD)
SCALE2 = SCALE * math.log2(math.e)
F32, BF16 = jnp.float32, jnp.bfloat16


def dot(a, b, ca=1, cb=0):
    return lax.dot_general(a, b, (((ca,), (cb,)), ((), ())), preferred_element_type=F32)


def kernel(
    n_dp,
    q_in,
    k_in,
    v_in,
    g_in,
    h_in,
    dq_out,
    dk_out,
    dv_out,
    wk_out,
    wv_out,
    q_buf,
    g_buf,
    kv_buf,
    q_t,
    g_t,
    e_buf,
    p_buf,
    m_buf,
    acc,
    dq_buf,
    core_send,
    core_recv,
    x_send,
    x_recv,
    fin,
    h_buf,
    kvg,
    wc_send,
    wc_recv,
    w_send,
    w_recv,
    w_res,
    s_q,
    s_g,
    s_kv,
    s_fw,
    s_h,
    s_dq,
    s_core,
    s_x,
    s_fin,
    s_a,
    s_wc,
    s_w,
    r_q,
    r_g,
    r_kv,
    r_fw,
    r_h,
    r_dq,
    r_core,
    r_x,
    r_fin,
    r_a,
    r_wc,
    r_w,
    o_sem,
):
    me_dp = lax.axis_index("dp")
    me = lax.axis_index("ctx")
    z, x, c = me // (NX * NC), (me // NC) % NX, me % NC
    oc = 1 - c
    tok = q_in.shape[0]
    blk = tok * NC
    heads = q_in.shape[1] // HD
    per_dev = heads // (NZ * NC)
    kv_cols = k_in.shape[1]
    rows = per_dev * blk

    def ctx_dev(zz, xx, cc):
        return (me_dp, (zz * NX + xx) * NC + cc)

    def remote(src, dst, ssem, rsem, dev):
        return pltpu.make_async_remote_copy(
            src_ref=src, dst_ref=dst, send_sem=ssem, recv_sem=rsem, device_id=dev, device_id_type=MESH
        )

    def wait_bytes(ref, sem):
        pltpu.make_async_copy(ref, ref, sem).wait()

    barrier = pltpu.get_barrier_semaphore()
    n_ctx = NZ * NX * NC
    for d in range(1, n_ctx):
        pl.semaphore_signal(barrier, inc=1, device_id=(me_dp, lax.rem(me + d, n_ctx)), device_id_type=MESH)
    for d in range(1, n_dp):
        pl.semaphore_signal(barrier, inc=1, device_id=(lax.rem(me_dp + d, n_dp), me), device_id_type=MESH)
    pl.semaphore_wait(barrier, n_ctx - 1 + n_dp - 1)

    my_block = z * NX + x
    share = h_in.shape[1] // n_dp

    for dz in range(NZ):
        gz = lax.rem(z + dz, NZ)
        cols = pl.ds(pl.multiple_of(gz * HD, HD), HD)
        for dx in range(NX):
            gx = lax.rem(x + dx, NX)
            for which, src in ((0, k_in), (1, v_in)):
                dst = kv_buf.at[my_block, c, which]
                if dz == 0 and dx == 0:
                    pltpu.make_async_copy(src.at[:, cols], dst, r_kv.at[my_block]).start()
                else:
                    remote(src.at[:, cols], dst, s_kv, r_kv.at[my_block], ctx_dev(gz, gx, c)).start()

    def send_queries(dz):
        gz = lax.rem(z + dz, NZ)
        for dc in range(NC):
            gc = lax.rem(c + dc, NC)
            for a in range(per_dev):
                col = ((gz * NC + gc) * per_dev + a) * HD
                cols = pl.ds(pl.multiple_of(col, HD), HD)
                spot = pl.ds(pl.multiple_of(c * tok, tok), tok)
                for src, buf, ssem, rsem in ((q_in, q_buf, s_q, r_q), (g_in, g_buf, s_g, r_g)):
                    dst = buf.at[z, a, spot, :]
                    if dz == 0 and dc == 0:
                        pltpu.make_async_copy(src.at[:, cols], dst, rsem.at[z]).start()
                    else:
                        remote(src.at[:, cols], dst, ssem, rsem.at[z], ctx_dev(gz, x, gc)).start()

    def send_near():
        send_queries(1)
        send_queries(NZ - 1)

    def send_far():
        send_queries(2)

    def send_hidden():
        for d in range(n_dp):
            gd = lax.rem(me_dp + d, n_dp)
            cols = pl.ds(pl.multiple_of(gd * share, HD), share)
            if d == 0:
                pltpu.make_async_copy(h_in.at[:, cols], h_buf.at[me_dp], r_h).start()
            else:
                remote(h_in.at[:, cols], h_buf.at[me_dp], s_h, r_h, (gd, me)).start()

    send_queries(0)
    send_near()
    acc[...] = jnp.zeros_like(acc)
    for d in range(NB):
        b = lax.rem(my_block + d, NB)
        wait_bytes(kv_buf.at[b, c], r_kv.at[b])
        remote(kv_buf.at[b, c], kv_buf.at[b, c], s_fw.at[b], r_fw.at[b], ctx_dev(z, x, oc)).start()
    send_far()
    for d in range(NB):
        b = lax.rem(my_block + d, NB)
        wait_bytes(kv_buf.at[b, oc], r_fw.at[b])

    def over_core(zz):
        both = pl.ds(zz * NX, NX)
        return remote(core_send.at[both], core_recv.at[both], s_core.at[zz], r_core.at[zz], ctx_dev(z, x, oc))

    def over_x(zz):
        return remote(x_send.at[zz], x_recv.at[zz], s_x.at[zz], r_x.at[zz], ctx_dev(z, 1 - x, c))

    def start_core(zz):
        for b in range(zz * NX, zz * NX + NX):
            core_send[b, 0] = (acc[0, b, oc] * SCALE).astype(BF16)
            core_send[b, 1] = acc[1, b, oc].astype(BF16)
        over_core(zz).start()

    def start_x(zz):
        over_core(zz).wait_recv()
        b = zz * NX + (1 - x)
        x_send[zz, 0] = (acc[0, b, c] * SCALE + core_recv[b, 0].astype(F32)).astype(BF16)
        x_send[zz, 1] = (acc[1, b, c] + core_recv[b, 1].astype(F32)).astype(BF16)
        over_x(zz).start()

    def finish(zz):
        over_x(zz).wait_recv()
        b = zz * NX + x
        fin[zz, 0] = (
            acc[0, b, c] * SCALE + core_recv[b, 0].astype(F32) + x_recv[zz, 0].astype(F32)
        ).astype(BF16)
        fin[zz, 1] = (acc[1, b, c] + core_recv[b, 1].astype(F32) + x_recv[zz, 1].astype(F32)).astype(BF16)
        for which in range(2):
            src = fin.at[zz, which]
            dst = kvg.at[which, me_dp, :, pl.ds(pl.multiple_of(z * HD, HD), HD)]

            @pl.when(z == zz)
            def _():
                pltpu.make_async_copy(src, dst, r_fin.at[which]).start()

            @pl.when(z != zz)
            def _():
                remote(src, dst, s_fin, r_fin.at[which], ctx_dev(zz, x, c)).start()

    def attend(step, carry):
        later = NZ - step
        zq = jnp.where(step == 0, z, jnp.where(later <= z, later - 1, later))
        zq = jnp.where(z == 1, lax.rem(step + 1, NZ), zq)
        last = zq * NX + x
        wait_bytes(q_buf.at[zq], r_q.at[zq])
        wait_bytes(g_buf.at[zq], r_g.at[zq])
        for a in range(per_dev):
            q_t[:, a * blk : (a + 1) * blk] = q_buf[zq, a].T
            g_t[:, a * blk : (a + 1) * blk] = g_buf[zq, a].T
        qt, gt = q_t[...], g_t[...]

        def first(b, carry, masked):
            top, total, delta = carry
            at = pl.ds(pl.multiple_of(b * blk, blk), blk)
            kb = kv_buf[b, :, 0].reshape(blk, HD)
            vb = kv_buf[b, :, 1].reshape(blk, HD)
            s = dot(kb, qt) * SCALE2
            if masked:
                key_id = lax.broadcasted_iota(jnp.int32, (blk, blk), 0)
                query_id = lax.broadcasted_iota(jnp.int32, (blk, blk), 1)
                seen = key_id <= query_id
                s = jnp.concatenate(
                    [jnp.where(seen, s[:, i * blk : (i + 1) * blk], -jnp.inf) for i in range(per_dev)], 1
                )
            dp = dot(vb, gt)
            new = jnp.maximum(top, jnp.max(s, axis=0, keepdims=True))
            shrink = jnp.exp2(top - new)
            e = jnp.exp2(s - new)
            total = total * shrink + jnp.sum(e, axis=0, keepdims=True)
            delta = delta * shrink + jnp.sum(e * dp, axis=0, keepdims=True)
            e_buf[at, :] = e.astype(BF16)
            p_buf[at, :] = dp
            m_buf[pl.ds(b, 1), :] = new
            return new, total, delta

        zero = jnp.zeros((1, rows), F32)
        stats = lax.fori_loop(0, last, lambda b, t: first(b, t, False), (zero - jnp.inf, zero, zero))
        top, total, delta = first(last, stats, True)
        inv = 1.0 / total
        delta = delta * inv

        def second(b, dqt):
            at = pl.ds(pl.multiple_of(b * blk, blk), blk)
            fix = jnp.exp2(m_buf[pl.ds(b, 1), :] - top) * inv
            prob = e_buf[at, :].astype(F32) * fix
            low = prob.astype(BF16)
            ds = (prob * (p_buf[at, :] - delta)).astype(BF16)
            kb = kv_buf[b, :, 0].reshape(blk, HD)
            acc[0, b] += dot(ds, q_buf[zq].reshape(rows, HD)).reshape(NC, tok, HD)
            acc[1, b] += dot(low, g_buf[zq].reshape(rows, HD)).reshape(NC, tok, HD)
            return dqt + dot(kb.T, ds)

        dqt = lax.fori_loop(0, last + 1, second, jnp.zeros((HD, rows), F32))
        for a in range(per_dev):
            dq_buf[zq, a] = (dqt[:, a * blk : (a + 1) * blk] * SCALE).T.astype(BF16)
        for gc in range(NC):
            mine = jnp.logical_and(zq == z, c == gc)
            for a in range(per_dev):
                col = ((z * NC + c) * per_dev + a) * HD
                cols = pl.ds(pl.multiple_of(col, HD), HD)
                src = dq_buf.at[zq, a, gc * tok : (gc + 1) * tok, :]

                @pl.when(mine)
                def _():
                    pltpu.make_async_copy(src, dq_out.at[:, cols], r_dq).start()

                @pl.when(jnp.logical_not(mine))
                def _():
                    remote(src, dq_out.at[:, cols], s_dq, r_dq, ctx_dev(zq, x, gc)).start()

        pl.when(step == 0)(send_hidden)

        @pl.when(step == 2)
        def _():
            start_core(NZ - 1)
            start_core(NZ - 2)
            start_x(NZ - 1)

        return carry

    lax.fori_loop(0, NZ, attend, 0)
    start_core(0)
    start_core(1)
    start_x(2)
    start_x(0)
    start_x(1)
    for zz in range(NZ - 1, -1, -1):
        finish(zz)

    half = tok // 2
    y, xl = me_dp // 2, me_dp % 2
    n_y = n_dp // 2
    up_y, down_y, far_y = lax.rem(y + 1, n_y), lax.rem(y + n_y - 1, n_y), lax.rem(y + 2, n_y)
    partner, up, down = y * 2 + (1 - xl), up_y * 2 + xl, down_y * 2 + xl
    up_p, down_p = up_y * 2 + (1 - xl), down_y * 2 + (1 - xl)
    low_half, high_half = pl.ds(0, half), pl.ds(half, half)
    every = pl.ds(0, tok)

    def pass_on(h, source, part, to, n):
        spot = kvg.at[h, source, part, :]
        return remote(spot, spot, s_a.at[h, n], r_a.at[h, n], (to, me))

    def hop(h, n):
        return (
            lambda: pass_on(h, me_dp, every, partner, 0),
            lambda: pass_on(h, me_dp, every, up, 1),
            lambda: pass_on(h, me_dp, every, down, 2),
            lambda: pass_on(h, partner, every, up, 3),
            lambda: pass_on(h, partner, every, down, 4),
            lambda: pass_on(h, down, low_half, up, 5),
            lambda: pass_on(h, up, high_half, down, 6),
            lambda: pass_on(h, down_p, low_half, up, 7),
            lambda: pass_on(h, up_p, high_half, down, 8),
        )[n]()

    def arrived(h, n):
        far, far_p = far_y * 2 + xl, far_y * 2 + (1 - xl)
        source, part = (
            (partner, every),
            (down, every),
            (up, every),
            (down_p, every),
            (up_p, every),
            (far, low_half),
            (far, high_half),
            (far_p, low_half),
            (far_p, high_half),
        )[n]
        wait_bytes(kvg.at[h, source, part, :], r_a.at[h, n])

    def own(h):
        wait_bytes(kvg.at[h, me_dp], r_fin.at[h])
        for n in range(3):
            hop(h, n).start()
        out = pltpu.make_async_copy(kvg.at[h, me_dp], (dk_out, dv_out)[h], o_sem.at[h])
        out.start()

    def relay(h, n, sends):
        arrived(h, n)
        for m in sends:
            hop(h, m).start()

    out_rows = share // (NB * NC)
    n_tok = n_dp * tok

    def project(h):
        cols = slice(h * kv_cols, (h + 1) * kv_cols)
        grads = kvg[h].reshape(n_tok, kv_cols)
        step_rows = share // NZ
        for i in range(NZ):
            at = slice(i * step_rows, (i + 1) * step_rows)
            p_buf[at, cols] = dot(e_buf[at, 0:n_tok], grads)
        for b in range(NB):
            at = pl.ds(pl.multiple_of((b * NC + oc) * out_rows, out_rows), out_rows)
            wc_send[h, b] = p_buf[at, cols].astype(BF16)
        w_core(h).start()

    def w_core(h):
        return remote(wc_send.at[h], wc_recv.at[h], s_wc.at[h], r_wc.at[h], ctx_dev(z, x, oc))

    def partial_sum(h, b):
        at = pl.ds(pl.multiple_of((b * NC + c) * out_rows, out_rows), out_rows)
        return p_buf[at, h * kv_cols : (h + 1) * kv_cols] + wc_recv[h, b].astype(F32)

    def spread(h):
        w_core(h).wait_recv()
        for d in range(1, NB):
            b = lax.rem(my_block + d, NB)
            w_send[h, b] = partial_sum(h, b).astype(BF16)
            dev = ctx_dev(b // NX, lax.rem(b, NX), c)
            remote(w_send.at[h, b], w_recv.at[h, my_block], s_w.at[h], r_w.at[h, my_block], dev).start()

    def collect(h):
        total = partial_sum(h, my_block)
        for d in range(1, NB):
            b = lax.rem(my_block + d, NB)
            wait_bytes(w_recv.at[h, b], r_w.at[h, b])
            total = total + w_recv[h, b].astype(F32)
        w_res[h] = total
        pltpu.make_async_copy(w_res.at[h], (wk_out, wv_out)[h], o_sem.at[2 + h]).start()

    own(0)
    wait_bytes(h_buf, r_h)
    for d in range(0, n_dp, 2):
        e_buf[0:share, d * tok : (d + 2) * tok] = h_buf[d : d + 2].reshape(2 * tok, share).T
    relay(0, 0, (3, 4))
    own(1)
    relay(0, 1, (5,))
    relay(0, 2, (6,))
    relay(1, 0, (3, 4))
    relay(0, 3, (7,))
    relay(0, 4, (8,))
    relay(1, 1, (5,))
    relay(1, 2, (6,))
    for n in range(5, 9):
        arrived(0, n)
    project(0)
    relay(1, 3, (7,))
    relay(1, 4, (8,))
    spread(0)
    for n in range(5, 9):
        arrived(1, n)
    project(1)
    spread(1)
    collect(0)
    collect(1)

    wait_bytes(dq_out, r_dq)
    part = heads - per_dev
    wait_bytes(q_in.at[:, : part * HD], s_q)
    wait_bytes(g_in.at[:, : part * HD], s_g)
    wait_bytes(q_in.at[:, : part * HD], s_dq)
    wait_bytes(q_in.at[:, : (NB - 1) * 2 * HD], s_kv)
    for b in range(NB):
        wait_bytes(kv_buf.at[b, c], s_fw.at[b])
    wait_bytes(h_in.at[:, : (n_dp - 1) * share], s_h)
    for zz in range(NZ):
        over_core(zz).wait_send()
        over_x(zz).wait_send()
    wait_bytes(fin.at[pl.ds(0, NZ - 1)], s_fin)
    for h in range(2):
        for n in range(9):
            hop(h, n).wait_send()
        w_core(h).wait_send()
        wait_bytes(w_send.at[h, pl.ds(0, NB - 1)], s_w.at[h])
        wait_bytes(kvg.at[h, me_dp], o_sem.at[h])
        wait_bytes(w_res.at[h], o_sem.at[2 + h])


def copy_out(*refs):
    n = len(refs) // 2
    for i in range(n):
        refs[n + i][...] = refs[i][...]


def on_device(n_dp, queries, keys, values, out_grad, hidden):
    tok, width = queries.shape
    kv_cols = keys.shape[1]
    blk = tok * NC
    per_dev = width // HD // (NZ * NC)
    rows = per_dev * blk
    share = hidden.shape[1] // n_dp
    out_rows = share // (NZ * NX * NC)
    dma = pltpu.SemaphoreType.DMA
    any_spec = pl.BlockSpec(memory_space=pl.ANY)
    assert n_dp * tok <= rows and share <= NB * blk and 2 * kv_cols <= rows and n_dp == 8
    shapes = [
        jax.ShapeDtypeStruct(queries.shape, BF16),
        jax.ShapeDtypeStruct(keys.shape, BF16),
        jax.ShapeDtypeStruct(values.shape, BF16),
        jax.ShapeDtypeStruct((out_rows, kv_cols), F32),
        jax.ShapeDtypeStruct((out_rows, kv_cols), F32),
    ]
    results = pl.pallas_call(
        functools.partial(kernel, n_dp),
        out_shape=shapes,
        in_specs=[any_spec] * 5,
        out_specs=[any_spec] * 5,
        scratch_shapes=[
            pltpu.VMEM((NZ, per_dev, blk, HD), BF16),
            pltpu.VMEM((NZ, per_dev, blk, HD), BF16),
            pltpu.VMEM((NB, NC, 2, tok, HD), BF16),
            pltpu.VMEM((HD, rows), BF16),
            pltpu.VMEM((HD, rows), BF16),
            pltpu.VMEM((NB * blk, rows), BF16),
            pltpu.VMEM((NB * blk, rows), F32),
            pltpu.VMEM((NB, rows), F32),
            pltpu.VMEM((2, NB, NC, tok, HD), F32),
            pltpu.VMEM((NZ, per_dev, blk, HD), BF16),
            pltpu.VMEM((NB, 2, tok, HD), BF16),
            pltpu.VMEM((NB, 2, tok, HD), BF16),
            pltpu.VMEM((NZ, 2, tok, HD), BF16),
            pltpu.VMEM((NZ, 2, tok, HD), BF16),
            pltpu.VMEM((NZ, 2, tok, HD), BF16),
            pltpu.VMEM((n_dp, tok, share), BF16),
            pltpu.VMEM((2, n_dp, tok, kv_cols), BF16),
            pltpu.VMEM((2, NB, out_rows, kv_cols), BF16),
            pltpu.VMEM((2, NB, out_rows, kv_cols), BF16),
            pltpu.VMEM((2, NB, out_rows, kv_cols), BF16),
            pltpu.VMEM((2, NB, out_rows, kv_cols), BF16),
            pltpu.VMEM((2, out_rows, kv_cols), F32),
            dma,
            dma,
            dma,
            dma((NB,)),
            dma,
            dma,
            dma((NZ,)),
            dma((NZ,)),
            dma,
            dma((2, 9)),
            dma((2,)),
            dma((2,)),
            dma((NZ,)),
            dma((NZ,)),
            dma((NB,)),
            dma((NB,)),
            dma,
            dma,
            dma((NZ,)),
            dma((NZ,)),
            dma((2,)),
            dma((2, 9)),
            dma((2,)),
            dma((2, NB)),
            dma((4,)),
        ],
        compiler_params=pltpu.CompilerParams(
            collective_id=0, has_side_effects=True, vmem_limit_bytes=60 * 1024 * 1024
        ),
        cost_estimate=pl.CostEstimate(
            flops=40_000_000_000, bytes_accessed=20_000_000, transcendentals=10_000_000
        ),
        name="attention_backward",
    )(queries, keys, values, out_grad, hidden)
    steps = 4
    specs = [pl.BlockSpec((a.shape[0] // steps, a.shape[1]), lambda i: (i, 0)) for a in shapes]
    return pl.pallas_call(
        copy_out,
        grid=(steps,),
        out_shape=shapes,
        in_specs=specs,
        out_specs=specs,
        cost_estimate=pl.CostEstimate(flops=0, bytes_accessed=4_500_000, transcendentals=0),
        name="copy_out",
    )(*results)


def solution(mesh):
    spec = P(("dp", "ctx"), None)
    return jax.shard_map(
        functools.partial(on_device, mesh.shape["dp"]),
        mesh=mesh,
        in_specs=(spec,) * 5,
        out_specs=(spec,) * 5,
        check_vma=False,
    )
```

```python
import functools
import math

import jax
import jax.numpy as jnp
from jax import lax
from jax.experimental import pallas as pl
from jax.experimental.pallas import tpu as pltpu
from jax.sharding import PartitionSpec as P

MESH = pl.DeviceIdType.MESH
HD = 128
NZ, NX, NC = 4, 2, 2
NB = NZ * NX
SCALE = 1.0 / math.sqrt(HD)
SCALE2 = SCALE * math.log2(math.e)
F32, BF16 = jnp.float32, jnp.bfloat16


def dot(a, b, ca=1, cb=0):
    return lax.dot_general(a, b, (((ca,), (cb,)), ((), ())), preferred_element_type=F32)


def kernel(
    n_dp,
    q_in,
    k_in,
    v_in,
    g_in,
    h_in,
    dq_out,
    dk_out,
    dv_out,
    wk_out,
    wv_out,
    q_buf,
    g_buf,
    kv_buf,
    q_t,
    g_t,
    e_buf,
    p_buf,
    m_buf,
    acc,
    dq_acc,
    core_send,
    core_recv,
    x_send,
    x_recv,
    fin,
    h_buf,
    kvg,
    wc_recv,
    w_recv,
    w_res,
    s_q,
    s_g,
    s_kv,
    s_fw,
    s_h,
    s_dq,
    s_core,
    s_x,
    s_fin,
    s_a,
    s_wc,
    s_w,
    r_q,
    r_g,
    r_kv,
    r_fw,
    r_h,
    r_dq,
    r_core,
    r_x,
    r_fin,
    r_a,
    r_wc,
    r_w,
    o_sem,
):
    me_dp = lax.axis_index("dp")
    me = lax.axis_index("ctx")
    z, x, c = me // (NX * NC), (me // NC) % NX, me % NC
    oc = 1 - c
    tok = q_in.shape[0]
    blk = tok * NC
    heads = q_in.shape[1] // HD
    per_dev = heads // (NZ * NC)
    kv_cols = k_in.shape[1]
    rows = per_dev * blk

    def ctx_dev(zz, xx, cc):
        return (me_dp, (zz * NX + xx) * NC + cc)

    def remote(src, dst, ssem, rsem, dev):
        return pltpu.make_async_remote_copy(
            src_ref=src, dst_ref=dst, send_sem=ssem, recv_sem=rsem, device_id=dev, device_id_type=MESH
        )

    def wait_bytes(ref, sem):
        pltpu.make_async_copy(ref, ref, sem).wait()

    barrier = pltpu.get_barrier_semaphore()
    n_ctx = NZ * NX * NC
    for d in range(1, n_ctx):
        pl.semaphore_signal(barrier, inc=1, device_id=(me_dp, lax.rem(me + d, n_ctx)), device_id_type=MESH)
    for d in range(1, n_dp):
        pl.semaphore_signal(barrier, inc=1, device_id=(lax.rem(me_dp + d, n_dp), me), device_id_type=MESH)
    pl.semaphore_wait(barrier, n_ctx - 1 + n_dp - 1)

    my_block = z * NX + x
    share = h_in.shape[1] // n_dp

    for dz in range(NZ):
        gz = lax.rem(z + dz, NZ)
        cols = pl.ds(pl.multiple_of(gz * HD, HD), HD)
        for dx in range(NX):
            gx = lax.rem(x + dx, NX)
            for which, src in ((0, k_in), (1, v_in)):
                dst = kv_buf.at[my_block, c, which]
                if dz == 0 and dx == 0:
                    pltpu.make_async_copy(src.at[:, cols], dst, r_kv.at[my_block]).start()
                else:
                    remote(src.at[:, cols], dst, s_kv, r_kv.at[my_block], ctx_dev(gz, gx, c)).start()

    def send_queries(dz):
        gz = lax.rem(z + dz, NZ)
        for dc in range(NC):
            gc = lax.rem(c + dc, NC)
            for a in range(per_dev):
                col = ((gz * NC + gc) * per_dev + a) * HD
                cols = pl.ds(pl.multiple_of(col, HD), HD)
                spot = pl.ds(pl.multiple_of(c * tok, tok), tok)
                for src, buf, ssem, rsem in ((q_in, q_buf, s_q, r_q), (g_in, g_buf, s_g, r_g)):
                    dst = buf.at[z, a, spot, :]
                    if dz == 0 and dc == 0:
                        pltpu.make_async_copy(src.at[:, cols], dst, rsem.at[z]).start()
                    else:
                        remote(src.at[:, cols], dst, ssem, rsem.at[z], ctx_dev(gz, x, gc)).start()

    def send_near():
        send_queries(1)
        send_queries(NZ - 1)

    def send_far():
        send_queries(2)

    def send_hidden():
        for d in range(n_dp):
            gd = lax.rem(me_dp + d, n_dp)
            cols = pl.ds(pl.multiple_of(gd * share, HD), share)
            if d == 0:
                pltpu.make_async_copy(h_in.at[:, cols], h_buf.at[me_dp], r_h).start()
            else:
                remote(h_in.at[:, cols], h_buf.at[me_dp], s_h, r_h, (gd, me)).start()

    send_queries(0)
    send_near()
    acc[...] = jnp.zeros_like(acc)
    for d in range(NB):
        b = lax.rem(my_block + d, NB)
        wait_bytes(kv_buf.at[b, c], r_kv.at[b])
        remote(kv_buf.at[b, c], kv_buf.at[b, c], s_fw.at[b], r_fw.at[b], ctx_dev(z, x, oc)).start()
    send_far()
    for d in range(NB):
        b = lax.rem(my_block + d, NB)
        wait_bytes(kv_buf.at[b, oc], r_fw.at[b])

    def over_core(zz):
        both = pl.ds(zz * NX, NX)
        return remote(core_send.at[both], core_recv.at[both], s_core.at[zz], r_core.at[zz], ctx_dev(z, x, oc))

    def over_x(zz):
        return remote(x_send.at[zz], x_recv.at[zz], s_x.at[zz], r_x.at[zz], ctx_dev(z, 1 - x, c))

    def start_core(zz):
        for b in range(zz * NX, zz * NX + NX):
            core_send[b, 0] = (acc[0, b, oc] * SCALE).astype(BF16)
            core_send[b, 1] = acc[1, b, oc].astype(BF16)
        over_core(zz).start()

    def start_x(zz):
        over_core(zz).wait_recv()
        b = zz * NX + (1 - x)
        x_send[zz, 0] = (acc[0, b, c] * SCALE + core_recv[b, 0].astype(F32)).astype(BF16)
        x_send[zz, 1] = (acc[1, b, c] + core_recv[b, 1].astype(F32)).astype(BF16)
        over_x(zz).start()

    def finish(zz):
        over_x(zz).wait_recv()
        b = zz * NX + x
        fin[zz, 0] = (
            acc[0, b, c] * SCALE + core_recv[b, 0].astype(F32) + x_recv[zz, 0].astype(F32)
        ).astype(BF16)
        fin[zz, 1] = (acc[1, b, c] + core_recv[b, 1].astype(F32) + x_recv[zz, 1].astype(F32)).astype(BF16)
        for which in range(2):
            src = fin.at[zz, which]
            dst = kvg.at[which, me_dp, :, pl.ds(pl.multiple_of(z * HD, HD), HD)]

            @pl.when(z == zz)
            def _():
                pltpu.make_async_copy(src, dst, r_fin.at[which]).start()

            @pl.when(z != zz)
            def _():
                remote(src, dst, s_fin, r_fin.at[which], ctx_dev(zz, x, c)).start()

    def attend(step, carry):
        later = NZ - step
        zq = jnp.where(step == 0, z, jnp.where(later <= z, later - 1, later))
        zq = jnp.where(z == 1, lax.rem(step + 1, NZ), zq)
        last = zq * NX + x
        wait_bytes(q_buf.at[zq], r_q.at[zq])
        wait_bytes(g_buf.at[zq], r_g.at[zq])
        for a in range(per_dev):
            q_t[:, a * blk : (a + 1) * blk] = q_buf[zq, a].T
            g_t[:, a * blk : (a + 1) * blk] = g_buf[zq, a].T
        qt, gt = q_t[...], g_t[...]

        def first(b, carry, masked):
            top, total, delta = carry
            at = pl.ds(pl.multiple_of(b * blk, blk), blk)
            kb = kv_buf[b, :, 0].reshape(blk, HD)
            vb = kv_buf[b, :, 1].reshape(blk, HD)
            s = dot(kb, qt) * SCALE2
            if masked:
                key_id = lax.broadcasted_iota(jnp.int32, (blk, blk), 0)
                query_id = lax.broadcasted_iota(jnp.int32, (blk, blk), 1)
                seen = key_id <= query_id
                s = jnp.concatenate(
                    [jnp.where(seen, s[:, i * blk : (i + 1) * blk], -jnp.inf) for i in range(per_dev)], 1
                )
            dp = dot(vb, gt)
            new = jnp.maximum(top, jnp.max(s, axis=0, keepdims=True))
            shrink = jnp.exp2(top - new)
            e = jnp.exp2(s - new)
            total = total * shrink + jnp.sum(e, axis=0, keepdims=True)
            delta = delta * shrink + jnp.sum(e * dp, axis=0, keepdims=True)
            e_buf[at, :] = e.astype(BF16)
            p_buf[at, :] = dp
            m_buf[pl.ds(b, 1), :] = new
            return new, total, delta

        zero = jnp.zeros((1, rows), F32)
        stats = lax.fori_loop(0, last, lambda b, t: first(b, t, False), (zero - jnp.inf, zero, zero))
        top, total, delta = first(last, stats, True)
        inv = 1.0 / total
        delta = delta * inv

        def second(b, n):
            lows, grads = [], []
            for i in range(n):
                at = pl.ds(pl.multiple_of((b + i) * blk, blk), blk)
                fix = jnp.exp2(m_buf[pl.ds(b + i, 1), :] - top) * inv
                prob = e_buf[at, :].astype(F32) * fix
                lows.append(prob.astype(BF16))
                grads.append((prob * (p_buf[at, :] - delta)).astype(BF16))
            low, ds = jnp.concatenate(lows, 0), jnp.concatenate(grads, 0)
            some = pl.ds(b, n)
            kb = kv_buf[some, :, 0].reshape(n * blk, HD)
            acc[0, some] += dot(ds, q_buf[zq].reshape(rows, HD)).reshape(n, NC, tok, HD)
            acc[1, some] += dot(low, g_buf[zq].reshape(rows, HD)).reshape(n, NC, tok, HD)
            dq_acc[...] += dot(kb.T, ds)

        dq_acc[...] = jnp.zeros_like(dq_acc)

        def pair(i, carry):
            second(2 * i, 2)
            return carry

        lax.fori_loop(0, (last + 1) // 2, pair, 0)

        @pl.when(x == 0)
        def _():
            second(last, 1)

        for a in range(per_dev):
            q_buf[zq, a] = (dq_acc[:, a * blk : (a + 1) * blk] * SCALE).T.astype(BF16)
        for gc in range(NC):
            mine = jnp.logical_and(zq == z, c == gc)
            for a in range(per_dev):
                col = ((z * NC + c) * per_dev + a) * HD
                cols = pl.ds(pl.multiple_of(col, HD), HD)
                src = q_buf.at[zq, a, gc * tok : (gc + 1) * tok, :]

                @pl.when(mine)
                def _():
                    pltpu.make_async_copy(src, dq_out.at[:, cols], r_dq).start()

                @pl.when(jnp.logical_not(mine))
                def _():
                    remote(src, dq_out.at[:, cols], s_dq, r_dq, ctx_dev(zq, x, gc)).start()

        pl.when(step == 0)(send_hidden)

        @pl.when(step == 2)
        def _():
            start_core(NZ - 1)
            start_core(NZ - 2)
            start_x(NZ - 1)

        return carry

    lax.fori_loop(0, NZ, attend, 0)
    start_core(0)
    start_core(1)
    start_x(2)
    start_x(0)
    start_x(1)
    for zz in range(NZ - 1, -1, -1):
        finish(zz)

    half = tok // 2
    y, xl = me_dp // 2, me_dp % 2
    n_y = n_dp // 2
    up_y, down_y, far_y = lax.rem(y + 1, n_y), lax.rem(y + n_y - 1, n_y), lax.rem(y + 2, n_y)
    partner, up, down = y * 2 + (1 - xl), up_y * 2 + xl, down_y * 2 + xl
    up_p, down_p = up_y * 2 + (1 - xl), down_y * 2 + (1 - xl)
    low_half, high_half = pl.ds(0, half), pl.ds(half, half)
    every = pl.ds(0, tok)

    def pass_on(h, source, part, to, n):
        spot = kvg.at[h, source, part, :]
        return remote(spot, spot, s_a.at[h, n], r_a.at[h, n], (to, me))

    def hop(h, n):
        return (
            lambda: pass_on(h, me_dp, every, partner, 0),
            lambda: pass_on(h, me_dp, every, up, 1),
            lambda: pass_on(h, me_dp, every, down, 2),
            lambda: pass_on(h, partner, every, up, 3),
            lambda: pass_on(h, partner, every, down, 4),
            lambda: pass_on(h, down, low_half, up, 5),
            lambda: pass_on(h, up, high_half, down, 6),
            lambda: pass_on(h, down_p, low_half, up, 7),
            lambda: pass_on(h, up_p, high_half, down, 8),
        )[n]()

    def arrived(h, n):
        far, far_p = far_y * 2 + xl, far_y * 2 + (1 - xl)
        source, part = (
            (partner, every),
            (down, every),
            (up, every),
            (down_p, every),
            (up_p, every),
            (far, low_half),
            (far, high_half),
            (far_p, low_half),
            (far_p, high_half),
        )[n]
        wait_bytes(kvg.at[h, source, part, :], r_a.at[h, n])

    def own(h):
        wait_bytes(kvg.at[h, me_dp], r_fin.at[h])
        for n in range(3):
            hop(h, n).start()
        out = pltpu.make_async_copy(kvg.at[h, me_dp], (dk_out, dv_out)[h], o_sem.at[h])
        out.start()

    def relay(h, n, sends):
        arrived(h, n)
        for m in sends:
            hop(h, m).start()

    out_rows = share // (NB * NC)
    n_tok = n_dp * tok

    def outgoing(h, n):
        return h_buf.at[:, n * out_rows : (n + 1) * out_rows, h * kv_cols : (h + 1) * kv_cols]

    def project(h):
        cols = slice(h * kv_cols, (h + 1) * kv_cols)
        grads = kvg[h].reshape(n_tok, kv_cols)
        step_rows = share // NZ
        for i in range(NZ):
            at = slice(i * step_rows, (i + 1) * step_rows)
            p_buf[at, cols] = dot(e_buf[at, 0:n_tok], grads)
        for b in range(NB):
            at = pl.ds(pl.multiple_of((b * NC + oc) * out_rows, out_rows), out_rows)
            outgoing(h, 0)[b] = p_buf[at, cols].astype(BF16)
        w_core(h).start()

    def w_core(h):
        return remote(outgoing(h, 0), wc_recv.at[h], s_wc.at[h], r_wc.at[h], ctx_dev(z, x, oc))

    def partial_sum(h, b):
        at = pl.ds(pl.multiple_of((b * NC + c) * out_rows, out_rows), out_rows)
        return p_buf[at, h * kv_cols : (h + 1) * kv_cols] + wc_recv[h, b].astype(F32)

    def spread(h):
        w_core(h).wait_recv()
        for d in range(1, NB):
            b = lax.rem(my_block + d, NB)
            outgoing(h, 1)[b] = partial_sum(h, b).astype(BF16)
            dev = ctx_dev(b // NX, lax.rem(b, NX), c)
            remote(outgoing(h, 1).at[b], w_recv.at[h, my_block], s_w.at[h], r_w.at[h, my_block], dev).start()

    def collect(h):
        total = partial_sum(h, my_block)
        for d in range(1, NB):
            b = lax.rem(my_block + d, NB)
            wait_bytes(w_recv.at[h, b], r_w.at[h, b])
            total = total + w_recv[h, b].astype(F32)
        w_res[h] = total
        pltpu.make_async_copy(w_res.at[h], (wk_out, wv_out)[h], o_sem.at[2 + h]).start()

    own(0)
    wait_bytes(h_buf, r_h)
    for d in range(0, n_dp, 2):
        e_buf[0:share, d * tok : (d + 2) * tok] = h_buf[d : d + 2].reshape(2 * tok, share).T
    relay(0, 0, (3, 4))
    own(1)
    relay(0, 1, (5,))
    relay(0, 2, (6,))
    relay(1, 0, (3, 4))
    relay(0, 3, (7,))
    relay(0, 4, (8,))
    relay(1, 1, (5,))
    relay(1, 2, (6,))
    for n in range(5, 9):
        arrived(0, n)
    project(0)
    relay(1, 3, (7,))
    relay(1, 4, (8,))
    spread(0)
    for n in range(5, 9):
        arrived(1, n)
    project(1)
    spread(1)
    collect(0)
    collect(1)

    wait_bytes(dq_out, r_dq)
    part = heads - per_dev
    wait_bytes(q_in.at[:, : part * HD], s_q)
    wait_bytes(g_in.at[:, : part * HD], s_g)
    wait_bytes(q_in.at[:, : part * HD], s_dq)
    wait_bytes(q_in.at[:, : (NB - 1) * 2 * HD], s_kv)
    for b in range(NB):
        wait_bytes(kv_buf.at[b, c], s_fw.at[b])
    wait_bytes(h_in.at[:, : (n_dp - 1) * share], s_h)
    for zz in range(NZ):
        over_core(zz).wait_send()
        over_x(zz).wait_send()
    wait_bytes(fin.at[pl.ds(0, NZ - 1)], s_fin)
    for h in range(2):
        for n in range(9):
            hop(h, n).wait_send()
        w_core(h).wait_send()
        wait_bytes(w_recv.at[h, pl.ds(0, NB - 1)], s_w.at[h])
        wait_bytes(kvg.at[h, me_dp], o_sem.at[h])
        wait_bytes(w_res.at[h], o_sem.at[2 + h])


def copy_out(*refs):
    n = len(refs) // 2
    for i in range(n):
        refs[n + i][...] = refs[i][...]


def on_device(n_dp, queries, keys, values, out_grad, hidden):
    tok, width = queries.shape
    kv_cols = keys.shape[1]
    blk = tok * NC
    per_dev = width // HD // (NZ * NC)
    rows = per_dev * blk
    share = hidden.shape[1] // n_dp
    out_rows = share // (NZ * NX * NC)
    dma = pltpu.SemaphoreType.DMA
    any_spec = pl.BlockSpec(memory_space=pl.ANY)
    assert n_dp * tok <= rows and share <= NB * blk and 2 * kv_cols <= rows and n_dp == NB == 8
    shapes = [
        jax.ShapeDtypeStruct(queries.shape, BF16),
        jax.ShapeDtypeStruct(keys.shape, BF16),
        jax.ShapeDtypeStruct(values.shape, BF16),
        jax.ShapeDtypeStruct((out_rows, kv_cols), F32),
        jax.ShapeDtypeStruct((out_rows, kv_cols), F32),
    ]
    results = pl.pallas_call(
        functools.partial(kernel, n_dp),
        out_shape=shapes,
        in_specs=[any_spec] * 5,
        out_specs=[any_spec] * 5,
        scratch_shapes=[
            pltpu.VMEM((NZ, per_dev, blk, HD), BF16),
            pltpu.VMEM((NZ, per_dev, blk, HD), BF16),
            pltpu.VMEM((NB, NC, 2, tok, HD), BF16),
            pltpu.VMEM((HD, rows), BF16),
            pltpu.VMEM((HD, rows), BF16),
            pltpu.VMEM((NB * blk, rows), BF16),
            pltpu.VMEM((NB * blk, rows), F32),
            pltpu.VMEM((NB, rows), F32),
            pltpu.VMEM((2, NB, NC, tok, HD), F32),
            pltpu.VMEM((HD, rows), F32),
            pltpu.VMEM((NB, 2, tok, HD), BF16),
            pltpu.VMEM((NB, 2, tok, HD), BF16),
            pltpu.VMEM((NZ, 2, tok, HD), BF16),
            pltpu.VMEM((NZ, 2, tok, HD), BF16),
            pltpu.VMEM((NZ, 2, tok, HD), BF16),
            pltpu.VMEM((n_dp, tok, share), BF16),
            pltpu.VMEM((2, n_dp, tok, kv_cols), BF16),
            pltpu.VMEM((2, NB, out_rows, kv_cols), BF16),
            pltpu.VMEM((2, NB, out_rows, kv_cols), BF16),
            pltpu.VMEM((2, out_rows, kv_cols), F32),
            dma,
            dma,
            dma,
            dma((NB,)),
            dma,
            dma,
            dma((NZ,)),
            dma((NZ,)),
            dma,
            dma((2, 9)),
            dma((2,)),
            dma((2,)),
            dma((NZ,)),
            dma((NZ,)),
            dma((NB,)),
            dma((NB,)),
            dma,
            dma,
            dma((NZ,)),
            dma((NZ,)),
            dma((2,)),
            dma((2, 9)),
            dma((2,)),
            dma((2, NB)),
            dma((4,)),
        ],
        compiler_params=pltpu.CompilerParams(
            collective_id=0, has_side_effects=True, vmem_limit_bytes=60 * 1024 * 1024
        ),
        cost_estimate=pl.CostEstimate(
            flops=40_000_000_000, bytes_accessed=20_000_000, transcendentals=10_000_000
        ),
        name="attention_backward",
    )(queries, keys, values, out_grad, hidden)
    steps = 4
    specs = [pl.BlockSpec((a.shape[0] // steps, a.shape[1]), lambda i: (i, 0)) for a in shapes]
    return pl.pallas_call(
        copy_out,
        grid=(steps,),
        out_shape=shapes,
        in_specs=specs,
        out_specs=specs,
        cost_estimate=pl.CostEstimate(flops=0, bytes_accessed=4_500_000, transcendentals=0),
        name="copy_out",
    )(*results)


def solution(mesh):
    spec = P(("dp", "ctx"), None)
    return jax.shard_map(
        functools.partial(on_device, mesh.shape["dp"]),
        mesh=mesh,
        in_specs=(spec,) * 5,
        out_specs=(spec,) * 5,
        check_vma=False,
    )
```

```python
import functools
import math

import jax
import jax.numpy as jnp
from jax import lax
from jax.experimental import pallas as pl
from jax.experimental.pallas import tpu as pltpu
from jax.sharding import PartitionSpec as P

MESH = pl.DeviceIdType.MESH
HD = 128
NZ, NX, NC = 4, 2, 2
NB = NZ * NX
SCALE = 1.0 / math.sqrt(HD)
SCALE2 = SCALE * math.log2(math.e)
F32, BF16 = jnp.float32, jnp.bfloat16


def dot(a, b, ca=1, cb=0):
    return lax.dot_general(a, b, (((ca,), (cb,)), ((), ())), preferred_element_type=F32)


def kernel(
    n_dp,
    q_in,
    k_in,
    v_in,
    g_in,
    h_in,
    dq_out,
    dk_out,
    dv_out,
    wk_out,
    wv_out,
    q_buf,
    g_buf,
    kv_buf,
    q_t,
    g_t,
    e_buf,
    p_buf,
    m_buf,
    acc,
    dq_acc,
    core_send,
    core_recv,
    x_send,
    x_recv,
    fin,
    h_buf,
    kvg,
    wc_recv,
    w_recv,
    w_res,
    s_q,
    s_g,
    s_kv,
    s_fw,
    s_h,
    s_dq,
    s_core,
    s_x,
    s_fin,
    s_a,
    s_wc,
    s_w,
    r_q,
    r_g,
    r_kv,
    r_fw,
    r_h,
    r_dq,
    r_core,
    r_x,
    r_fin,
    r_a,
    r_wc,
    r_w,
    o_sem,
):
    me_dp = lax.axis_index("dp")
    me = lax.axis_index("ctx")
    z, x, c = me // (NX * NC), (me // NC) % NX, me % NC
    oc = 1 - c
    tok = q_in.shape[0]
    blk = tok * NC
    heads = q_in.shape[1] // HD
    per_dev = heads // (NZ * NC)
    kv_cols = k_in.shape[1]
    rows = per_dev * blk

    def ctx_dev(zz, xx, cc):
        return (me_dp, (zz * NX + xx) * NC + cc)

    def remote(src, dst, ssem, rsem, dev):
        return pltpu.make_async_remote_copy(
            src_ref=src, dst_ref=dst, send_sem=ssem, recv_sem=rsem, device_id=dev, device_id_type=MESH
        )

    def wait_bytes(ref, sem):
        pltpu.make_async_copy(ref, ref, sem).wait()

    barrier = pltpu.get_barrier_semaphore()
    n_ctx = NZ * NX * NC
    for d in range(1, n_ctx):
        pl.semaphore_signal(barrier, inc=1, device_id=(me_dp, lax.rem(me + d, n_ctx)), device_id_type=MESH)
    for d in range(1, n_dp):
        pl.semaphore_signal(barrier, inc=1, device_id=(lax.rem(me_dp + d, n_dp), me), device_id_type=MESH)
    pl.semaphore_wait(barrier, n_ctx - 1 + n_dp - 1)

    my_block = z * NX + x
    share = h_in.shape[1] // n_dp

    for dz in range(NZ):
        gz = lax.rem(z + dz, NZ)
        cols = pl.ds(pl.multiple_of(gz * HD, HD), HD)
        for dx in range(NX):
            gx = lax.rem(x + dx, NX)
            for which, src in ((0, k_in), (1, v_in)):
                dst = kv_buf.at[my_block, c, which]
                if dz == 0 and dx == 0:
                    pltpu.make_async_copy(src.at[:, cols], dst, r_kv.at[my_block]).start()
                else:
                    remote(src.at[:, cols], dst, s_kv, r_kv.at[my_block], ctx_dev(gz, gx, c)).start()

    def send_queries(dz):
        gz = lax.rem(z + dz, NZ)
        for dc in range(NC):
            gc = lax.rem(c + dc, NC)
            for a in range(per_dev):
                col = ((gz * NC + gc) * per_dev + a) * HD
                cols = pl.ds(pl.multiple_of(col, HD), HD)
                spot = pl.ds(pl.multiple_of(c * tok, tok), tok)
                for src, buf, ssem, rsem in ((q_in, q_buf, s_q, r_q), (g_in, g_buf, s_g, r_g)):
                    dst = buf.at[z, a, spot, :]
                    if dz == 0 and dc == 0:
                        pltpu.make_async_copy(src.at[:, cols], dst, rsem.at[z]).start()
                    else:
                        remote(src.at[:, cols], dst, ssem, rsem.at[z], ctx_dev(gz, x, gc)).start()

    def send_near():
        send_queries(1)
        send_queries(NZ - 1)

    def send_far():
        send_queries(2)

    def send_hidden():
        for d in range(n_dp):
            gd = lax.rem(me_dp + d, n_dp)
            cols = pl.ds(pl.multiple_of(gd * share, HD), share)
            if d == 0:
                pltpu.make_async_copy(h_in.at[:, cols], h_buf.at[me_dp], r_h).start()
            else:
                remote(h_in.at[:, cols], h_buf.at[me_dp], s_h, r_h, (gd, me)).start()

    send_queries(0)
    send_near()
    acc[...] = jnp.zeros_like(acc)
    for d in range(NB):
        b = lax.rem(my_block + d, NB)
        wait_bytes(kv_buf.at[b, c], r_kv.at[b])
        remote(kv_buf.at[b, c], kv_buf.at[b, c], s_fw.at[b], r_fw.at[b], ctx_dev(z, x, oc)).start()
    send_far()
    for d in range(NB):
        b = lax.rem(my_block + d, NB)
        wait_bytes(kv_buf.at[b, oc], r_fw.at[b])

    def over_core(zz):
        both = pl.ds(zz * NX, NX)
        return remote(core_send.at[both], core_recv.at[both], s_core.at[zz], r_core.at[zz], ctx_dev(z, x, oc))

    def over_x(zz):
        return remote(x_send.at[zz], x_recv.at[zz], s_x.at[zz], r_x.at[zz], ctx_dev(z, 1 - x, c))

    def start_core(zz):
        for b in range(zz * NX, zz * NX + NX):
            core_send[b, 0] = (acc[0, b, oc] * SCALE).astype(BF16)
            core_send[b, 1] = acc[1, b, oc].astype(BF16)
        over_core(zz).start()

    def start_x(zz):
        over_core(zz).wait_recv()
        b = zz * NX + (1 - x)
        x_send[zz, 0] = (acc[0, b, c] * SCALE + core_recv[b, 0].astype(F32)).astype(BF16)
        x_send[zz, 1] = (acc[1, b, c] + core_recv[b, 1].astype(F32)).astype(BF16)
        over_x(zz).start()

    def finish(zz):
        over_x(zz).wait_recv()
        b = zz * NX + x
        fin[zz, 0] = (
            acc[0, b, c] * SCALE + core_recv[b, 0].astype(F32) + x_recv[zz, 0].astype(F32)
        ).astype(BF16)
        fin[zz, 1] = (acc[1, b, c] + core_recv[b, 1].astype(F32) + x_recv[zz, 1].astype(F32)).astype(BF16)
        for which in range(2):
            src = fin.at[zz, which]
            dst = kvg.at[which, me_dp, :, pl.ds(pl.multiple_of(z * HD, HD), HD)]

            @pl.when(z == zz)
            def _():
                pltpu.make_async_copy(src, dst, r_fin.at[which]).start()

            @pl.when(z != zz)
            def _():
                remote(src, dst, s_fin, r_fin.at[which], ctx_dev(zz, x, c)).start()

    def attend(step, carry):
        later = NZ - step
        zq = jnp.where(step == 0, z, jnp.where(later <= z, later - 1, later))
        zq = jnp.where(z == 1, lax.rem(step + 1, NZ), zq)
        last = zq * NX + x
        wait_bytes(q_buf.at[zq], r_q.at[zq])
        wait_bytes(g_buf.at[zq], r_g.at[zq])
        for a in range(per_dev):
            q_t[:, a * blk : (a + 1) * blk] = q_buf[zq, a].T
            g_t[:, a * blk : (a + 1) * blk] = g_buf[zq, a].T
        qt, gt = q_t[...], g_t[...]

        def first(b, carry, masked):
            top, total, delta = carry
            at = pl.ds(pl.multiple_of(b * blk, blk), blk)
            kb = kv_buf[b, :, 0].reshape(blk, HD)
            vb = kv_buf[b, :, 1].reshape(blk, HD)
            s = dot(kb, qt) * SCALE2
            if masked:
                key_id = lax.broadcasted_iota(jnp.int32, (blk, blk), 0)
                query_id = lax.broadcasted_iota(jnp.int32, (blk, blk), 1)
                seen = key_id <= query_id
                s = jnp.concatenate(
                    [jnp.where(seen, s[:, i * blk : (i + 1) * blk], -jnp.inf) for i in range(per_dev)], 1
                )
            dp = dot(vb, gt)
            new = jnp.maximum(top, jnp.max(s, axis=0, keepdims=True))
            shrink = jnp.exp2(top - new)
            e = jnp.exp2(s - new)
            total = total * shrink + jnp.sum(e, axis=0, keepdims=True)
            delta = delta * shrink + jnp.sum(e * dp, axis=0, keepdims=True)
            e_buf[at, :] = e.astype(BF16)
            p_buf[at, :] = dp
            m_buf[pl.ds(b, 1), :] = new
            return new, total, delta

        zero = jnp.zeros((1, rows), F32)
        stats = lax.fori_loop(0, last, lambda b, t: first(b, t, False), (zero - jnp.inf, zero, zero))
        top, total, delta = first(last, stats, True)
        inv = 1.0 / total
        delta = delta * inv

        def second(b, n):
            lows, grads = [], []
            for i in range(n):
                at = pl.ds(pl.multiple_of((b + i) * blk, blk), blk)
                fix = jnp.exp2(m_buf[pl.ds(b + i, 1), :] - top) * inv
                prob = e_buf[at, :].astype(F32) * fix
                lows.append(prob.astype(BF16))
                grads.append((prob * (p_buf[at, :] - delta)).astype(BF16))
            low, ds = jnp.concatenate(lows, 0), jnp.concatenate(grads, 0)
            some = pl.ds(b, n)
            kb = kv_buf[some, :, 0].reshape(n * blk, HD)
            acc[0, some] += dot(ds, q_buf[zq].reshape(rows, HD)).reshape(n, NC, tok, HD)
            acc[1, some] += dot(low, g_buf[zq].reshape(rows, HD)).reshape(n, NC, tok, HD)
            dq_acc[...] += dot(kb.T, ds)

        dq_acc[...] = jnp.zeros_like(dq_acc)

        def pair(i, carry):
            second(2 * i, 2)
            return carry

        lax.fori_loop(0, (last + 1) // 2, pair, 0)

        @pl.when(x == 0)
        def _():
            second(last, 1)

        for a in range(per_dev):
            q_buf[zq, a] = (dq_acc[:, a * blk : (a + 1) * blk] * SCALE).T.astype(BF16)
        for gc in range(NC):
            mine = jnp.logical_and(zq == z, c == gc)
            for a in range(per_dev):
                col = ((z * NC + c) * per_dev + a) * HD
                cols = pl.ds(pl.multiple_of(col, HD), HD)
                src = q_buf.at[zq, a, gc * tok : (gc + 1) * tok, :]

                @pl.when(mine)
                def _():
                    pltpu.make_async_copy(src, dq_out.at[:, cols], r_dq).start()

                @pl.when(jnp.logical_not(mine))
                def _():
                    remote(src, dq_out.at[:, cols], s_dq, r_dq, ctx_dev(zq, x, gc)).start()

        pl.when(step == 0)(send_hidden)

        @pl.when(step == 2)
        def _():
            start_core(NZ - 1)
            start_core(NZ - 2)
            start_x(NZ - 1)

        return carry

    lax.fori_loop(0, NZ, attend, 0)
    start_core(0)
    start_core(1)
    start_x(2)
    start_x(0)
    start_x(1)
    wait_bytes(h_buf, r_h)
    for zz in range(NZ - 1, -1, -1):
        finish(zz)
        if zz >= 2:
            for d in range(4 * (NZ - 1 - zz), 4 * (NZ - zz), 2):
                e_buf[0:share, d * tok : (d + 2) * tok] = h_buf[d : d + 2].reshape(2 * tok, share).T

    half = tok // 2
    y, xl = me_dp // 2, me_dp % 2
    n_y = n_dp // 2
    up_y, down_y, far_y = lax.rem(y + 1, n_y), lax.rem(y + n_y - 1, n_y), lax.rem(y + 2, n_y)
    partner, up, down = y * 2 + (1 - xl), up_y * 2 + xl, down_y * 2 + xl
    up_p, down_p = up_y * 2 + (1 - xl), down_y * 2 + (1 - xl)
    low_half, high_half = pl.ds(0, half), pl.ds(half, half)
    every = pl.ds(0, tok)

    def pass_on(h, source, part, to, n):
        spot = kvg.at[h, source, part, :]
        return remote(spot, spot, s_a.at[h, n], r_a.at[h, n], (to, me))

    def hop(h, n):
        return (
            lambda: pass_on(h, me_dp, every, partner, 0),
            lambda: pass_on(h, me_dp, every, up, 1),
            lambda: pass_on(h, me_dp, every, down, 2),
            lambda: pass_on(h, partner, every, up, 3) if h == 0 else pass_on(h, down, every, partner, 3),
            lambda: pass_on(h, partner, every, down, 4) if h == 1 else pass_on(h, up, every, partner, 4),
            lambda: pass_on(h, down, low_half, up, 5),
            lambda: pass_on(h, up, high_half, down, 6),
            lambda: pass_on(h, down_p, low_half, up, 7),
            lambda: pass_on(h, up_p, high_half, down, 8),
        )[n]()

    def arrived(h, n):
        far, far_p = far_y * 2 + xl, far_y * 2 + (1 - xl)
        source, part = (
            (partner, every),
            (down, every),
            (up, every),
            (down_p, every),
            (up_p, every),
            (far, low_half),
            (far, high_half),
            (far_p, low_half),
            (far_p, high_half),
        )[n]
        wait_bytes(kvg.at[h, source, part, :], r_a.at[h, n])

    def own(h):
        wait_bytes(kvg.at[h, me_dp], r_fin.at[h])
        for n in range(3):
            hop(h, n).start()
        out = pltpu.make_async_copy(kvg.at[h, me_dp], (dk_out, dv_out)[h], o_sem.at[h])
        out.start()

    def relay(h, n, sends):
        arrived(h, n)
        for m in sends:
            hop(h, m).start()

    out_rows = share // (NB * NC)
    n_tok = n_dp * tok

    def outgoing(h, n):
        return h_buf.at[:, n * out_rows : (n + 1) * out_rows, h * kv_cols : (h + 1) * kv_cols]

    def project(h):
        cols = slice(h * kv_cols, (h + 1) * kv_cols)
        grads = kvg[h].reshape(n_tok, kv_cols)
        step_rows = share // NZ
        for i in range(NZ):
            at = slice(i * step_rows, (i + 1) * step_rows)
            p_buf[at, cols] = dot(e_buf[at, 0:n_tok], grads)
        for b in range(NB):
            at = pl.ds(pl.multiple_of((b * NC + oc) * out_rows, out_rows), out_rows)
            outgoing(h, 0)[b] = p_buf[at, cols].astype(BF16)
        w_core(h).start()

    def w_core(h):
        return remote(outgoing(h, 0), wc_recv.at[h], s_wc.at[h], r_wc.at[h], ctx_dev(z, x, oc))

    def partial_sum(h, b):
        at = pl.ds(pl.multiple_of((b * NC + c) * out_rows, out_rows), out_rows)
        return p_buf[at, h * kv_cols : (h + 1) * kv_cols] + wc_recv[h, b].astype(F32)

    def spread(h):
        w_core(h).wait_recv()
        for d in range(1, NB):
            b = lax.rem(my_block + d, NB)
            outgoing(h, 1)[b] = partial_sum(h, b).astype(BF16)
            dev = ctx_dev(b // NX, lax.rem(b, NX), c)
            remote(outgoing(h, 1).at[b], w_recv.at[h, my_block], s_w.at[h], r_w.at[h, my_block], dev).start()

    def collect(h):
        total = partial_sum(h, my_block)
        for d in range(1, NB):
            b = lax.rem(my_block + d, NB)
            wait_bytes(w_recv.at[h, b], r_w.at[h, b])
            total = total + w_recv[h, b].astype(F32)
        w_res[h] = total
        pltpu.make_async_copy(w_res.at[h], (wk_out, wv_out)[h], o_sem.at[2 + h]).start()

    own(0)
    relay(0, 0, (3,))
    own(1)
    relay(0, 1, (5,))
    relay(0, 2, (6, 4))
    relay(1, 0, (4,))
    relay(0, 3, (7,))
    relay(1, 1, (5, 3))
    relay(1, 2, (6,))
    relay(0, 4, (8,))
    for n in range(5, 9):
        arrived(0, n)
    project(0)
    relay(1, 3, (7,))
    relay(1, 4, (8,))
    spread(0)
    for n in range(5, 9):
        arrived(1, n)
    project(1)
    spread(1)
    collect(0)
    collect(1)

    wait_bytes(dq_out, r_dq)
    part = heads - per_dev
    wait_bytes(q_in.at[:, : part * HD], s_q)
    wait_bytes(g_in.at[:, : part * HD], s_g)
    wait_bytes(q_in.at[:, : part * HD], s_dq)
    wait_bytes(q_in.at[:, : (NB - 1) * 2 * HD], s_kv)
    for b in range(NB):
        wait_bytes(kv_buf.at[b, c], s_fw.at[b])
    wait_bytes(h_in.at[:, : (n_dp - 1) * share], s_h)
    for zz in range(NZ):
        over_core(zz).wait_send()
        over_x(zz).wait_send()
    wait_bytes(fin.at[pl.ds(0, NZ - 1)], s_fin)
    for h in range(2):
        for n in range(9):
            hop(h, n).wait_send()
        w_core(h).wait_send()
        wait_bytes(w_recv.at[h, pl.ds(0, NB - 1)], s_w.at[h])
        wait_bytes(kvg.at[h, me_dp], o_sem.at[h])
        wait_bytes(w_res.at[h], o_sem.at[2 + h])


def copy_out(*refs):
    n = len(refs) // 2
    for i in range(n):
        refs[n + i][...] = refs[i][...]


def on_device(n_dp, queries, keys, values, out_grad, hidden):
    tok, width = queries.shape
    kv_cols = keys.shape[1]
    blk = tok * NC
    per_dev = width // HD // (NZ * NC)
    rows = per_dev * blk
    share = hidden.shape[1] // n_dp
    out_rows = share // (NZ * NX * NC)
    dma = pltpu.SemaphoreType.DMA
    any_spec = pl.BlockSpec(memory_space=pl.ANY)
    assert n_dp * tok <= rows and share <= NB * blk and 2 * kv_cols <= rows and n_dp == NB == 8
    shapes = [
        jax.ShapeDtypeStruct(queries.shape, BF16),
        jax.ShapeDtypeStruct(keys.shape, BF16),
        jax.ShapeDtypeStruct(values.shape, BF16),
        jax.ShapeDtypeStruct((out_rows, kv_cols), F32),
        jax.ShapeDtypeStruct((out_rows, kv_cols), F32),
    ]
    results = pl.pallas_call(
        functools.partial(kernel, n_dp),
        out_shape=shapes,
        in_specs=[any_spec] * 5,
        out_specs=[any_spec] * 5,
        scratch_shapes=[
            pltpu.VMEM((NZ, per_dev, blk, HD), BF16),
            pltpu.VMEM((NZ, per_dev, blk, HD), BF16),
            pltpu.VMEM((NB, NC, 2, tok, HD), BF16),
            pltpu.VMEM((HD, rows), BF16),
            pltpu.VMEM((HD, rows), BF16),
            pltpu.VMEM((NB * blk, rows), BF16),
            pltpu.VMEM((NB * blk, rows), F32),
            pltpu.VMEM((NB, rows), F32),
            pltpu.VMEM((2, NB, NC, tok, HD), F32),
            pltpu.VMEM((HD, rows), F32),
            pltpu.VMEM((NB, 2, tok, HD), BF16),
            pltpu.VMEM((NB, 2, tok, HD), BF16),
            pltpu.VMEM((NZ, 2, tok, HD), BF16),
            pltpu.VMEM((NZ, 2, tok, HD), BF16),
            pltpu.VMEM((NZ, 2, tok, HD), BF16),
            pltpu.VMEM((n_dp, tok, share), BF16),
            pltpu.VMEM((2, n_dp, tok, kv_cols), BF16),
            pltpu.VMEM((2, NB, out_rows, kv_cols), BF16),
            pltpu.VMEM((2, NB, out_rows, kv_cols), BF16),
            pltpu.VMEM((2, out_rows, kv_cols), F32),
            dma,
            dma,
            dma,
            dma((NB,)),
            dma,
            dma,
            dma((NZ,)),
            dma((NZ,)),
            dma,
            dma((2, 9)),
            dma((2,)),
            dma((2,)),
            dma((NZ,)),
            dma((NZ,)),
            dma((NB,)),
            dma((NB,)),
            dma,
            dma,
            dma((NZ,)),
            dma((NZ,)),
            dma((2,)),
            dma((2, 9)),
            dma((2,)),
            dma((2, NB)),
            dma((4,)),
        ],
        compiler_params=pltpu.CompilerParams(
            collective_id=0, has_side_effects=True, vmem_limit_bytes=60 * 1024 * 1024
        ),
        cost_estimate=pl.CostEstimate(
            flops=40_000_000_000, bytes_accessed=20_000_000, transcendentals=10_000_000
        ),
        name="attention_backward",
    )(queries, keys, values, out_grad, hidden)
    steps = 4
    specs = [pl.BlockSpec((a.shape[0] // steps, a.shape[1]), lambda i: (i, 0)) for a in shapes]
    return pl.pallas_call(
        copy_out,
        grid=(steps,),
        out_shape=shapes,
        in_specs=specs,
        out_specs=specs,
        cost_estimate=pl.CostEstimate(flops=0, bytes_accessed=4_500_000, transcendentals=0),
        name="copy_out",
    )(*results)


def solution(mesh):
    spec = P(("dp", "ctx"), None)
    return jax.shard_map(
        functools.partial(on_device, mesh.shape["dp"]),
        mesh=mesh,
        in_specs=(spec,) * 5,
        out_specs=(spec,) * 5,
        check_vma=False,
    )
```

```python
import functools
import math

import jax
import jax.numpy as jnp
from jax import lax
from jax.experimental import pallas as pl
from jax.experimental.pallas import tpu as pltpu
from jax.sharding import PartitionSpec as P

MESH = pl.DeviceIdType.MESH
HD = 128
NZ, NX, NC = 4, 2, 2
NB = NZ * NX
SCALE = 1.0 / math.sqrt(HD)
SCALE2 = SCALE * math.log2(math.e)
F32, BF16 = jnp.float32, jnp.bfloat16


def dot(a, b, ca=1, cb=0):
    return lax.dot_general(a, b, (((ca,), (cb,)), ((), ())), preferred_element_type=F32)


def kernel(
    n_dp,
    q_in,
    k_in,
    v_in,
    g_in,
    h_in,
    dq_out,
    dk_out,
    dv_out,
    wk_out,
    wv_out,
    q_buf,
    g_buf,
    kv_buf,
    q_t,
    g_t,
    e_buf,
    p_buf,
    m_buf,
    acc,
    dq_acc,
    core_send,
    core_recv,
    x_send,
    x_recv,
    fin,
    h_buf,
    kvg,
    wc_recv,
    w_recv,
    w_res,
    s_q,
    s_g,
    s_kv,
    s_fw,
    s_h,
    s_dq,
    s_core,
    s_x,
    s_fin,
    s_a,
    s_wc,
    s_w,
    r_q,
    r_g,
    r_kv,
    r_fw,
    r_h,
    r_dq,
    r_core,
    r_x,
    r_fin,
    r_a,
    r_wc,
    r_w,
    o_sem,
):
    me_dp = lax.axis_index("dp")
    me = lax.axis_index("ctx")
    z, x, c = me // (NX * NC), (me // NC) % NX, me % NC
    oc = 1 - c
    tok = q_in.shape[0]
    blk = tok * NC
    heads = q_in.shape[1] // HD
    per_dev = heads // (NZ * NC)
    kv_cols = k_in.shape[1]
    rows = per_dev * blk

    def ctx_dev(zz, xx, cc):
        return (me_dp, (zz * NX + xx) * NC + cc)

    def remote(src, dst, ssem, rsem, dev):
        return pltpu.make_async_remote_copy(
            src_ref=src, dst_ref=dst, send_sem=ssem, recv_sem=rsem, device_id=dev, device_id_type=MESH
        )

    def wait_bytes(ref, sem):
        pltpu.make_async_copy(ref, ref, sem).wait()

    barrier = pltpu.get_barrier_semaphore()
    n_ctx = NZ * NX * NC
    for d in range(1, n_ctx):
        pl.semaphore_signal(barrier, inc=1, device_id=(me_dp, lax.rem(me + d, n_ctx)), device_id_type=MESH)
    for d in range(1, n_dp):
        pl.semaphore_signal(barrier, inc=1, device_id=(lax.rem(me_dp + d, n_dp), me), device_id_type=MESH)
    pl.semaphore_wait(barrier, n_ctx - 1 + n_dp - 1)

    my_block = z * NX + x
    share = h_in.shape[1] // n_dp

    for dz in range(NZ):
        gz = lax.rem(z + dz, NZ)
        cols = pl.ds(pl.multiple_of(gz * HD, HD), HD)
        for dx in range(NX):
            gx = lax.rem(x + dx, NX)
            for which, src in ((0, k_in), (1, v_in)):
                dst = kv_buf.at[my_block, c, which]
                if dz == 0 and dx == 0:
                    pltpu.make_async_copy(src.at[:, cols], dst, r_kv.at[my_block]).start()
                else:
                    remote(src.at[:, cols], dst, s_kv, r_kv.at[my_block], ctx_dev(gz, gx, c)).start()

    def send_queries(dz):
        gz = lax.rem(z + dz, NZ)
        for dc in range(NC):
            gc = lax.rem(c + dc, NC)
            for a in range(per_dev):
                col = ((gz * NC + gc) * per_dev + a) * HD
                cols = pl.ds(pl.multiple_of(col, HD), HD)
                spot = pl.ds(pl.multiple_of(c * tok, tok), tok)
                for src, buf, ssem, rsem in ((q_in, q_buf, s_q, r_q), (g_in, g_buf, s_g, r_g)):
                    dst = buf.at[z, a, spot, :]
                    if dz == 0 and dc == 0:
                        pltpu.make_async_copy(src.at[:, cols], dst, rsem.at[z]).start()
                    else:
                        remote(src.at[:, cols], dst, ssem, rsem.at[z], ctx_dev(gz, x, gc)).start()

    def send_near():
        send_queries(1)
        send_queries(NZ - 1)

    def send_far():
        send_queries(2)

    def send_hidden():
        for d in range(n_dp):
            gd = lax.rem(me_dp + d, n_dp)
            cols = pl.ds(pl.multiple_of(gd * share, HD), share)
            if d == 0:
                pltpu.make_async_copy(h_in.at[:, cols], h_buf.at[me_dp], r_h).start()
            else:
                remote(h_in.at[:, cols], h_buf.at[me_dp], s_h, r_h, (gd, me)).start()

    send_queries(0)
    send_near()
    acc[...] = jnp.zeros_like(acc)
    for d in range(NB):
        b = lax.rem(my_block + d, NB)
        wait_bytes(kv_buf.at[b, c], r_kv.at[b])
        remote(kv_buf.at[b, c], kv_buf.at[b, c], s_fw.at[b], r_fw.at[b], ctx_dev(z, x, oc)).start()
    send_far()
    for d in range(NB):
        b = lax.rem(my_block + d, NB)
        wait_bytes(kv_buf.at[b, oc], r_fw.at[b])
    send_hidden()

    def over_core(zz):
        both = pl.ds(zz * NX, NX)
        return remote(core_send.at[both], core_recv.at[both], s_core.at[zz], r_core.at[zz], ctx_dev(z, x, oc))

    def over_x(zz):
        return remote(x_send.at[zz], x_recv.at[zz], s_x.at[zz], r_x.at[zz], ctx_dev(z, 1 - x, c))

    def start_core(zz):
        for b in range(zz * NX, zz * NX + NX):
            core_send[b, 0] = (acc[0, b, oc] * SCALE).astype(BF16)
            core_send[b, 1] = acc[1, b, oc].astype(BF16)
        over_core(zz).start()

    def start_x(zz):
        over_core(zz).wait_recv()
        b = zz * NX + (1 - x)
        x_send[zz, 0] = (acc[0, b, c] * SCALE + core_recv[b, 0].astype(F32)).astype(BF16)
        x_send[zz, 1] = (acc[1, b, c] + core_recv[b, 1].astype(F32)).astype(BF16)
        over_x(zz).start()

    def finish(zz):
        over_x(zz).wait_recv()
        b = zz * NX + x
        fin[zz, 0] = (
            acc[0, b, c] * SCALE + core_recv[b, 0].astype(F32) + x_recv[zz, 0].astype(F32)
        ).astype(BF16)
        fin[zz, 1] = (acc[1, b, c] + core_recv[b, 1].astype(F32) + x_recv[zz, 1].astype(F32)).astype(BF16)
        for which in range(2):
            src = fin.at[zz, which]
            dst = kvg.at[which, me_dp, :, pl.ds(pl.multiple_of(z * HD, HD), HD)]

            @pl.when(z == zz)
            def _():
                pltpu.make_async_copy(src, dst, r_fin.at[which]).start()

            @pl.when(z != zz)
            def _():
                remote(src, dst, s_fin, r_fin.at[which], ctx_dev(zz, x, c)).start()

    def attend(step, carry):
        later = NZ - step
        zq = jnp.where(step == 0, z, jnp.where(later <= z, later - 1, later))
        zq = jnp.where(z == 1, lax.rem(step + 1, NZ), zq)
        last = zq * NX + x
        wait_bytes(q_buf.at[zq], r_q.at[zq])
        wait_bytes(g_buf.at[zq], r_g.at[zq])
        for a in range(per_dev):
            q_t[:, a * blk : (a + 1) * blk] = q_buf[zq, a].T
            g_t[:, a * blk : (a + 1) * blk] = g_buf[zq, a].T
        qt, gt = q_t[...], g_t[...]

        def first(b, carry, masked):
            top, total, delta = carry
            at = pl.ds(pl.multiple_of(b * blk, blk), blk)
            kb = kv_buf[b, :, 0].reshape(blk, HD)
            vb = kv_buf[b, :, 1].reshape(blk, HD)
            s = dot(kb, qt) * SCALE2
            if masked:
                key_id = lax.broadcasted_iota(jnp.int32, (blk, blk), 0)
                query_id = lax.broadcasted_iota(jnp.int32, (blk, blk), 1)
                seen = key_id <= query_id
                s = jnp.concatenate(
                    [jnp.where(seen, s[:, i * blk : (i + 1) * blk], -jnp.inf) for i in range(per_dev)], 1
                )
            dp = dot(vb, gt)
            new = jnp.maximum(top, jnp.max(s, axis=0, keepdims=True))
            shrink = jnp.exp2(top - new)
            e = jnp.exp2(s - new)
            total = total * shrink + jnp.sum(e, axis=0, keepdims=True)
            delta = delta * shrink + jnp.sum(e * dp, axis=0, keepdims=True)
            e_buf[at, :] = e.astype(BF16)
            p_buf[at, :] = dp
            m_buf[pl.ds(b, 1), :] = new
            return new, total, delta

        zero = jnp.zeros((1, rows), F32)
        stats = lax.fori_loop(0, last, lambda b, t: first(b, t, False), (zero - jnp.inf, zero, zero))
        top, total, delta = first(last, stats, True)
        inv = 1.0 / total
        delta = delta * inv

        def second(b, n):
            lows, grads = [], []
            for i in range(n):
                at = pl.ds(pl.multiple_of((b + i) * blk, blk), blk)
                fix = jnp.exp2(m_buf[pl.ds(b + i, 1), :] - top) * inv
                prob = e_buf[at, :].astype(F32) * fix
                lows.append(prob.astype(BF16))
                grads.append((prob * (p_buf[at, :] - delta)).astype(BF16))
            low, ds = jnp.concatenate(lows, 0), jnp.concatenate(grads, 0)
            some = pl.ds(b, n)
            kb = kv_buf[some, :, 0].reshape(n * blk, HD)
            acc[0, some] += dot(ds, q_buf[zq].reshape(rows, HD)).reshape(n, NC, tok, HD)
            acc[1, some] += dot(low, g_buf[zq].reshape(rows, HD)).reshape(n, NC, tok, HD)
            dq_acc[...] += dot(kb.T, ds)

        dq_acc[...] = jnp.zeros_like(dq_acc)

        def pair(i, carry):
            second(2 * i, 2)
            return carry

        lax.fori_loop(0, (last + 1) // 2, pair, 0)

        @pl.when(x == 0)
        def _():
            second(last, 1)

        for a in range(per_dev):
            q_buf[zq, a] = (dq_acc[:, a * blk : (a + 1) * blk] * SCALE).T.astype(BF16)
        for gc in range(NC):
            mine = jnp.logical_and(zq == z, c == gc)
            for a in range(per_dev):
                col = ((z * NC + c) * per_dev + a) * HD
                cols = pl.ds(pl.multiple_of(col, HD), HD)
                src = q_buf.at[zq, a, gc * tok : (gc + 1) * tok, :]

                @pl.when(mine)
                def _():
                    pltpu.make_async_copy(src, dq_out.at[:, cols], r_dq).start()

                @pl.when(jnp.logical_not(mine))
                def _():
                    remote(src, dq_out.at[:, cols], s_dq, r_dq, ctx_dev(zq, x, gc)).start()

        @pl.when(step == 2)
        def _():
            start_core(NZ - 1)
            start_core(NZ - 2)
            start_x(NZ - 1)

        return carry

    lax.fori_loop(0, NZ, attend, 0)
    start_core(0)
    start_core(1)
    start_x(2)
    start_x(0)
    start_x(1)
    for zz in range(NZ - 1, -1, -1):
        finish(zz)
        if zz == NZ - 1:
            wait_bytes(h_buf, r_h)
        if zz >= 2:
            for d in range(4 * (NZ - 1 - zz), 4 * (NZ - zz), 2):
                e_buf[0:share, d * tok : (d + 2) * tok] = h_buf[d : d + 2].reshape(2 * tok, share).T

    half = tok // 2
    y, xl = me_dp // 2, me_dp % 2
    n_y = n_dp // 2
    up_y, down_y, far_y = lax.rem(y + 1, n_y), lax.rem(y + n_y - 1, n_y), lax.rem(y + 2, n_y)
    partner, up, down = y * 2 + (1 - xl), up_y * 2 + xl, down_y * 2 + xl
    up_p, down_p = up_y * 2 + (1 - xl), down_y * 2 + (1 - xl)
    low_half, high_half = pl.ds(0, half), pl.ds(half, half)
    every = pl.ds(0, tok)

    def pass_on(h, source, part, to, n):
        spot = kvg.at[h, source, part, :]
        return remote(spot, spot, s_a.at[h, n], r_a.at[h, n], (to, me))

    def hop(h, n):
        return (
            lambda: pass_on(h, me_dp, every, partner, 0),
            lambda: pass_on(h, me_dp, every, up, 1),
            lambda: pass_on(h, me_dp, every, down, 2),
            lambda: pass_on(h, partner, every, up, 3) if h == 0 else pass_on(h, down, every, partner, 3),
            lambda: pass_on(h, partner, every, down, 4) if h == 1 else pass_on(h, up, every, partner, 4),
            lambda: pass_on(h, down, low_half, up, 5),
            lambda: pass_on(h, up, high_half, down, 6),
            lambda: pass_on(h, down_p, low_half, up, 7),
            lambda: pass_on(h, up_p, high_half, down, 8),
        )[n]()

    def arrived(h, n):
        far, far_p = far_y * 2 + xl, far_y * 2 + (1 - xl)
        source, part = (
            (partner, every),
            (down, every),
            (up, every),
            (down_p, every),
            (up_p, every),
            (far, low_half),
            (far, high_half),
            (far_p, low_half),
            (far_p, high_half),
        )[n]
        wait_bytes(kvg.at[h, source, part, :], r_a.at[h, n])

    def own(h):
        wait_bytes(kvg.at[h, me_dp], r_fin.at[h])
        for n in range(3):
            hop(h, n).start()
        out = pltpu.make_async_copy(kvg.at[h, me_dp], (dk_out, dv_out)[h], o_sem.at[h])
        out.start()

    def relay(h, n, sends):
        arrived(h, n)
        for m in sends:
            hop(h, m).start()

    out_rows = share // (NB * NC)
    n_tok = n_dp * tok

    def outgoing(h, n):
        return h_buf.at[:, n * out_rows : (n + 1) * out_rows, h * kv_cols : (h + 1) * kv_cols]

    def project(h):
        cols = slice(h * kv_cols, (h + 1) * kv_cols)
        grads = kvg[h].reshape(n_tok, kv_cols)
        step_rows = share // NZ
        for i in range(NZ):
            at = slice(i * step_rows, (i + 1) * step_rows)
            p_buf[at, cols] = dot(e_buf[at, 0:n_tok], grads)
        for b in range(NB):
            at = pl.ds(pl.multiple_of((b * NC + oc) * out_rows, out_rows), out_rows)
            outgoing(h, 0)[b] = p_buf[at, cols].astype(BF16)
        w_core(h).start()

    def w_core(h):
        return remote(outgoing(h, 0), wc_recv.at[h], s_wc.at[h], r_wc.at[h], ctx_dev(z, x, oc))

    def partial_sum(h, b):
        at = pl.ds(pl.multiple_of((b * NC + c) * out_rows, out_rows), out_rows)
        return p_buf[at, h * kv_cols : (h + 1) * kv_cols] + wc_recv[h, b].astype(F32)

    def spread(h):
        w_core(h).wait_recv()
        for d in range(1, NB):
            b = lax.rem(my_block + d, NB)
            outgoing(h, 1)[b] = partial_sum(h, b).astype(BF16)
            dev = ctx_dev(b // NX, lax.rem(b, NX), c)
            remote(outgoing(h, 1).at[b], w_recv.at[h, my_block], s_w.at[h], r_w.at[h, my_block], dev).start()

    def collect(h):
        total = partial_sum(h, my_block)
        for d in range(1, NB):
            b = lax.rem(my_block + d, NB)
            wait_bytes(w_recv.at[h, b], r_w.at[h, b])
            total = total + w_recv[h, b].astype(F32)
        w_res[h] = total
        pltpu.make_async_copy(w_res.at[h], (wk_out, wv_out)[h], o_sem.at[2 + h]).start()

    own(0)
    relay(0, 0, (3,))
    own(1)
    relay(0, 1, (5,))
    relay(0, 2, (6, 4))
    relay(1, 0, (4,))
    relay(0, 3, (7,))
    relay(1, 1, (5, 3))
    relay(1, 2, (6,))
    relay(0, 4, (8,))
    for n in range(5, 9):
        arrived(0, n)
    project(0)
    relay(1, 3, (7,))
    relay(1, 4, (8,))
    spread(0)
    for n in range(5, 9):
        arrived(1, n)
    project(1)
    spread(1)
    collect(0)
    collect(1)

    wait_bytes(dq_out, r_dq)
    part = heads - per_dev
    wait_bytes(q_in.at[:, : part * HD], s_q)
    wait_bytes(g_in.at[:, : part * HD], s_g)
    wait_bytes(q_in.at[:, : part * HD], s_dq)
    wait_bytes(q_in.at[:, : (NB - 1) * 2 * HD], s_kv)
    for b in range(NB):
        wait_bytes(kv_buf.at[b, c], s_fw.at[b])
    wait_bytes(h_in.at[:, : (n_dp - 1) * share], s_h)
    for zz in range(NZ):
        over_core(zz).wait_send()
        over_x(zz).wait_send()
    wait_bytes(fin.at[pl.ds(0, NZ - 1)], s_fin)
    for h in range(2):
        for n in range(9):
            hop(h, n).wait_send()
        w_core(h).wait_send()
        wait_bytes(w_recv.at[h, pl.ds(0, NB - 1)], s_w.at[h])
        wait_bytes(kvg.at[h, me_dp], o_sem.at[h])
        wait_bytes(w_res.at[h], o_sem.at[2 + h])


def copy_out(*refs):
    n = len(refs) // 2
    for i in range(n):
        refs[n + i][...] = refs[i][...]


def on_device(n_dp, queries, keys, values, out_grad, hidden):
    tok, width = queries.shape
    kv_cols = keys.shape[1]
    blk = tok * NC
    per_dev = width // HD // (NZ * NC)
    rows = per_dev * blk
    share = hidden.shape[1] // n_dp
    out_rows = share // (NZ * NX * NC)
    dma = pltpu.SemaphoreType.DMA
    any_spec = pl.BlockSpec(memory_space=pl.ANY)
    assert n_dp * tok <= rows and share <= NB * blk and 2 * kv_cols <= rows and n_dp == NB == 8
    shapes = [
        jax.ShapeDtypeStruct(queries.shape, BF16),
        jax.ShapeDtypeStruct(keys.shape, BF16),
        jax.ShapeDtypeStruct(values.shape, BF16),
        jax.ShapeDtypeStruct((out_rows, kv_cols), F32),
        jax.ShapeDtypeStruct((out_rows, kv_cols), F32),
    ]
    results = pl.pallas_call(
        functools.partial(kernel, n_dp),
        out_shape=shapes,
        in_specs=[any_spec] * 5,
        out_specs=[any_spec] * 5,
        scratch_shapes=[
            pltpu.VMEM((NZ, per_dev, blk, HD), BF16),
            pltpu.VMEM((NZ, per_dev, blk, HD), BF16),
            pltpu.VMEM((NB, NC, 2, tok, HD), BF16),
            pltpu.VMEM((HD, rows), BF16),
            pltpu.VMEM((HD, rows), BF16),
            pltpu.VMEM((NB * blk, rows), BF16),
            pltpu.VMEM((NB * blk, rows), F32),
            pltpu.VMEM((NB, rows), F32),
            pltpu.VMEM((2, NB, NC, tok, HD), F32),
            pltpu.VMEM((HD, rows), F32),
            pltpu.VMEM((NB, 2, tok, HD), BF16),
            pltpu.VMEM((NB, 2, tok, HD), BF16),
            pltpu.VMEM((NZ, 2, tok, HD), BF16),
            pltpu.VMEM((NZ, 2, tok, HD), BF16),
            pltpu.VMEM((NZ, 2, tok, HD), BF16),
            pltpu.VMEM((n_dp, tok, share), BF16),
            pltpu.VMEM((2, n_dp, tok, kv_cols), BF16),
            pltpu.VMEM((2, NB, out_rows, kv_cols), BF16),
            pltpu.VMEM((2, NB, out_rows, kv_cols), BF16),
            pltpu.VMEM((2, out_rows, kv_cols), F32),
            dma,
            dma,
            dma,
            dma((NB,)),
            dma,
            dma,
            dma((NZ,)),
            dma((NZ,)),
            dma,
            dma((2, 9)),
            dma((2,)),
            dma((2,)),
            dma((NZ,)),
            dma((NZ,)),
            dma((NB,)),
            dma((NB,)),
            dma,
            dma,
            dma((NZ,)),
            dma((NZ,)),
            dma((2,)),
            dma((2, 9)),
            dma((2,)),
            dma((2, NB)),
            dma((4,)),
        ],
        compiler_params=pltpu.CompilerParams(
            collective_id=0, has_side_effects=True, vmem_limit_bytes=60 * 1024 * 1024
        ),
        cost_estimate=pl.CostEstimate(
            flops=40_000_000_000, bytes_accessed=20_000_000, transcendentals=10_000_000
        ),
        name="attention_backward",
    )(queries, keys, values, out_grad, hidden)
    steps = 4
    specs = [pl.BlockSpec((a.shape[0] // steps, a.shape[1]), lambda i: (i, 0)) for a in shapes]
    return pl.pallas_call(
        copy_out,
        grid=(steps,),
        out_shape=shapes,
        in_specs=specs,
        out_specs=specs,
        cost_estimate=pl.CostEstimate(flops=0, bytes_accessed=4_500_000, transcendentals=0),
        name="copy_out",
    )(*results)


def solution(mesh):
    spec = P(("dp", "ctx"), None)
    return jax.shard_map(
        functools.partial(on_device, mesh.shape["dp"]),
        mesh=mesh,
        in_specs=(spec,) * 5,
        out_specs=(spec,) * 5,
        check_vma=False,
    )
```

```python
import functools
import math

import jax
import jax.numpy as jnp
from jax import lax
from jax.experimental import pallas as pl
from jax.experimental.pallas import tpu as pltpu
from jax.sharding import PartitionSpec as P

MESH = pl.DeviceIdType.MESH
HD = 128
NZ, NX, NC = 4, 2, 2
NB = NZ * NX
SCALE = 1.0 / math.sqrt(HD)
SCALE2 = SCALE * math.log2(math.e)
F32, BF16 = jnp.float32, jnp.bfloat16


def dot(a, b, ca=1, cb=0):
    return lax.dot_general(a, b, (((ca,), (cb,)), ((), ())), preferred_element_type=F32)


def kernel(
    n_dp,
    q_in,
    k_in,
    v_in,
    g_in,
    h_in,
    dq_out,
    dk_out,
    dv_out,
    wk_out,
    wv_out,
    q_buf,
    g_buf,
    kv_buf,
    q_t,
    g_t,
    e_buf,
    p_buf,
    m_buf,
    acc,
    dq_acc,
    core_send,
    core_recv,
    x_send,
    x_recv,
    fin,
    h_buf,
    kvg,
    wc_recv,
    w_recv,
    w_res,
    s_q,
    s_g,
    s_kv,
    s_fw,
    s_h,
    s_dq,
    s_core,
    s_x,
    s_fin,
    s_a,
    s_wc,
    s_w,
    r_q,
    r_g,
    r_kv,
    r_fw,
    r_h,
    r_dq,
    r_core,
    r_x,
    r_fin,
    r_a,
    r_wc,
    r_w,
    o_sem,
):
    me_dp = lax.axis_index("dp")
    me = lax.axis_index("ctx")
    z, x, c = me // (NX * NC), (me // NC) % NX, me % NC
    oc = 1 - c
    tok = q_in.shape[0]
    blk = tok * NC
    heads = q_in.shape[1] // HD
    per_dev = heads // (NZ * NC)
    kv_cols = k_in.shape[1]
    rows = per_dev * blk

    def ctx_dev(zz, xx, cc):
        return (me_dp, (zz * NX + xx) * NC + cc)

    def remote(src, dst, ssem, rsem, dev):
        return pltpu.make_async_remote_copy(
            src_ref=src, dst_ref=dst, send_sem=ssem, recv_sem=rsem, device_id=dev, device_id_type=MESH
        )

    def wait_bytes(ref, sem):
        pltpu.make_async_copy(ref, ref, sem).wait()

    barrier = pltpu.get_barrier_semaphore()
    n_ctx = NZ * NX * NC
    for d in range(1, n_ctx):
        pl.semaphore_signal(barrier, inc=1, device_id=(me_dp, lax.rem(me + d, n_ctx)), device_id_type=MESH)
    for d in range(1, n_dp):
        pl.semaphore_signal(barrier, inc=1, device_id=(lax.rem(me_dp + d, n_dp), me), device_id_type=MESH)
    pl.semaphore_wait(barrier, n_ctx - 1 + n_dp - 1)

    my_block = z * NX + x
    share = h_in.shape[1] // n_dp

    for dz in range(NZ):
        gz = lax.rem(z + dz, NZ)
        cols = pl.ds(pl.multiple_of(gz * HD, HD), HD)
        for dx in range(NX):
            gx = lax.rem(x + dx, NX)
            for which, src in ((0, k_in), (1, v_in)):
                dst = kv_buf.at[my_block, c, which]
                if dz == 0 and dx == 0:
                    pltpu.make_async_copy(src.at[:, cols], dst, r_kv.at[my_block]).start()
                else:
                    remote(src.at[:, cols], dst, s_kv, r_kv.at[my_block], ctx_dev(gz, gx, c)).start()

    def send_queries(dz):
        gz = lax.rem(z + dz, NZ)
        for dc in range(NC):
            gc = lax.rem(c + dc, NC)
            for a in range(per_dev):
                col = ((gz * NC + gc) * per_dev + a) * HD
                cols = pl.ds(pl.multiple_of(col, HD), HD)
                spot = pl.ds(pl.multiple_of(c * tok, tok), tok)
                for src, buf, ssem, rsem in ((q_in, q_buf, s_q, r_q), (g_in, g_buf, s_g, r_g)):
                    dst = buf.at[z, a, spot, :]
                    if dz == 0 and dc == 0:
                        pltpu.make_async_copy(src.at[:, cols], dst, rsem.at[z]).start()
                    else:
                        remote(src.at[:, cols], dst, ssem, rsem.at[z], ctx_dev(gz, x, gc)).start()

    def send_near():
        send_queries(1)
        send_queries(NZ - 1)

    def send_far():
        send_queries(2)

    def send_hidden():
        for d in range(n_dp):
            gd = lax.rem(me_dp + d, n_dp)
            cols = pl.ds(pl.multiple_of(gd * share, HD), share)
            if d == 0:
                pltpu.make_async_copy(h_in.at[:, cols], h_buf.at[me_dp], r_h).start()
            else:
                remote(h_in.at[:, cols], h_buf.at[me_dp], s_h, r_h, (gd, me)).start()

    send_queries(0)
    send_near()
    acc[...] = jnp.zeros_like(acc)
    for d in range(NB):
        b = lax.rem(my_block + d, NB)
        wait_bytes(kv_buf.at[b, c], r_kv.at[b])
        remote(kv_buf.at[b, c], kv_buf.at[b, c], s_fw.at[b], r_fw.at[b], ctx_dev(z, x, oc)).start()
    send_far()
    for d in range(NB):
        b = lax.rem(my_block + d, NB)
        wait_bytes(kv_buf.at[b, oc], r_fw.at[b])
    send_hidden()

    def over_core(zz):
        both = pl.ds(zz * NX, NX)
        return remote(core_send.at[both], core_recv.at[both], s_core.at[zz], r_core.at[zz], ctx_dev(z, x, oc))

    def over_x(zz):
        return remote(x_send.at[zz], x_recv.at[zz], s_x.at[zz], r_x.at[zz], ctx_dev(z, 1 - x, c))

    def start_core(zz):
        for b in range(zz * NX, zz * NX + NX):
            core_send[b, 0] = (acc[0, b, oc] * SCALE).astype(BF16)
            core_send[b, 1] = acc[1, b, oc].astype(BF16)
        over_core(zz).start()

    def start_x(zz):
        over_core(zz).wait_recv()
        b = zz * NX + (1 - x)
        x_send[zz, 0] = (acc[0, b, c] * SCALE + core_recv[b, 0].astype(F32)).astype(BF16)
        x_send[zz, 1] = (acc[1, b, c] + core_recv[b, 1].astype(F32)).astype(BF16)
        over_x(zz).start()

    def finish(zz):
        over_x(zz).wait_recv()
        b = zz * NX + x
        fin[zz, 0] = (
            acc[0, b, c] * SCALE + core_recv[b, 0].astype(F32) + x_recv[zz, 0].astype(F32)
        ).astype(BF16)
        fin[zz, 1] = (acc[1, b, c] + core_recv[b, 1].astype(F32) + x_recv[zz, 1].astype(F32)).astype(BF16)
        for which in range(2):
            src = fin.at[zz, which]
            dst = kvg.at[which, me_dp, :, pl.ds(pl.multiple_of(z * HD, HD), HD)]

            @pl.when(z == zz)
            def _():
                pltpu.make_async_copy(src, dst, r_fin.at[which]).start()

            @pl.when(z != zz)
            def _():
                remote(src, dst, s_fin, r_fin.at[which], ctx_dev(zz, x, c)).start()

    def attend(step, carry):
        later = NZ - step
        zq = jnp.where(step == 0, z, jnp.where(later <= z, later - 1, later))
        zq = jnp.where(z == 1, lax.rem(step + 1, NZ), zq)
        last = zq * NX + x
        wait_bytes(q_buf.at[zq], r_q.at[zq])
        wait_bytes(g_buf.at[zq], r_g.at[zq])
        for a in range(per_dev):
            q_t[:, a * blk : (a + 1) * blk] = q_buf[zq, a].T
            g_t[:, a * blk : (a + 1) * blk] = g_buf[zq, a].T
        qt, gt = q_t[...], g_t[...]

        def first(b, carry, masked):
            top, total, delta = carry
            at = pl.ds(pl.multiple_of(b * blk, blk), blk)
            kb = kv_buf[b, :, 0].reshape(blk, HD)
            vb = kv_buf[b, :, 1].reshape(blk, HD)
            s = dot(kb, qt) * SCALE2
            if masked:
                key_id = lax.broadcasted_iota(jnp.int32, (blk, blk), 0)
                query_id = lax.broadcasted_iota(jnp.int32, (blk, blk), 1)
                seen = key_id <= query_id
                s = jnp.concatenate(
                    [jnp.where(seen, s[:, i * blk : (i + 1) * blk], -jnp.inf) for i in range(per_dev)], 1
                )
            dp = dot(vb, gt)
            new = jnp.maximum(top, jnp.max(s, axis=0, keepdims=True))
            shrink = jnp.exp2(top - new)
            e = jnp.exp2(s - new)
            total = total * shrink + jnp.sum(e, axis=0, keepdims=True)
            delta = delta * shrink + jnp.sum(e * dp, axis=0, keepdims=True)
            e_buf[at, :] = e.astype(BF16)
            p_buf[at, :] = dp
            m_buf[pl.ds(b, 1), :] = new
            return new, total, delta

        zero = jnp.zeros((1, rows), F32)
        stats = lax.fori_loop(0, last, lambda b, t: first(b, t, False), (zero - jnp.inf, zero, zero))
        top, total, delta = first(last, stats, True)
        inv = 1.0 / total
        delta = delta * inv

        def second(b, n):
            lows, grads = [], []
            for i in range(n):
                at = pl.ds(pl.multiple_of((b + i) * blk, blk), blk)
                fix = jnp.exp2(m_buf[pl.ds(b + i, 1), :] - top) * inv
                prob = e_buf[at, :].astype(F32) * fix
                lows.append(prob.astype(BF16))
                grads.append((prob * (p_buf[at, :] - delta)).astype(BF16))
            low, ds = jnp.concatenate(lows, 0), jnp.concatenate(grads, 0)
            some = pl.ds(b, n)
            kb = kv_buf[some, :, 0].reshape(n * blk, HD)
            acc[0, some] += dot(ds, q_buf[zq].reshape(rows, HD)).reshape(n, NC, tok, HD)
            acc[1, some] += dot(low, g_buf[zq].reshape(rows, HD)).reshape(n, NC, tok, HD)
            dq_acc[...] += dot(kb.T, ds)

        dq_acc[...] = jnp.zeros_like(dq_acc)

        def pair(i, carry):
            second(2 * i, 2)
            return carry

        lax.fori_loop(0, (last + 1) // 2, pair, 0)

        @pl.when(x == 0)
        def _():
            second(last, 1)

        for a in range(per_dev):
            q_buf[zq, a] = (dq_acc[:, a * blk : (a + 1) * blk] * SCALE).T.astype(BF16)
        for gc in range(NC):
            mine = jnp.logical_and(zq == z, c == gc)
            for a in range(per_dev):
                col = ((z * NC + c) * per_dev + a) * HD
                cols = pl.ds(pl.multiple_of(col, HD), HD)
                src = q_buf.at[zq, a, gc * tok : (gc + 1) * tok, :]

                @pl.when(mine)
                def _():
                    pltpu.make_async_copy(src, dq_out.at[:, cols], r_dq).start()

                @pl.when(jnp.logical_not(mine))
                def _():
                    remote(src, dq_out.at[:, cols], s_dq, r_dq, ctx_dev(zq, x, gc)).start()

        @pl.when(step == 2)
        def _():
            start_core(NZ - 1)
            start_core(NZ - 2)
            start_x(NZ - 1)

        return carry

    lax.fori_loop(0, NZ, attend, 0)
    start_core(0)
    start_core(1)
    start_x(2)
    start_x(0)
    start_x(1)
    for zz in range(NZ - 1, -1, -1):
        finish(zz)
        if zz == NZ - 1:
            wait_bytes(h_buf, r_h)
        if zz >= 2:
            for d in range(4 * (NZ - 1 - zz), 4 * (NZ - zz), 2):
                e_buf[0:share, d * tok : (d + 2) * tok] = h_buf[d : d + 2].reshape(2 * tok, share).T

    half = tok // 2
    y, xl = me_dp // 2, me_dp % 2
    n_y = n_dp // 2
    up_y, down_y, far_y = lax.rem(y + 1, n_y), lax.rem(y + n_y - 1, n_y), lax.rem(y + 2, n_y)
    partner, up, down = y * 2 + (1 - xl), up_y * 2 + xl, down_y * 2 + xl
    up_p, down_p = up_y * 2 + (1 - xl), down_y * 2 + (1 - xl)
    low_half, high_half = pl.ds(0, half), pl.ds(half, half)
    every = pl.ds(0, tok)

    def pass_on(h, source, part, to, n):
        spot = kvg.at[h, source, part, :]
        return remote(spot, spot, s_a.at[h, n], r_a.at[h, n], (to, me))

    def hop(h, n):
        return (
            lambda: pass_on(h, me_dp, every, partner, 0),
            lambda: pass_on(h, me_dp, every, up, 1),
            lambda: pass_on(h, me_dp, every, down, 2),
            lambda: pass_on(h, partner, every, up, 3) if h == 0 else pass_on(h, down, every, partner, 3),
            lambda: pass_on(h, partner, every, down, 4) if h == 1 else pass_on(h, up, every, partner, 4),
            lambda: pass_on(h, down, low_half, up, 5),
            lambda: pass_on(h, up, high_half, down, 6),
            lambda: pass_on(h, down_p, low_half, up, 7),
            lambda: pass_on(h, up_p, high_half, down, 8),
        )[n]()

    def arrived(h, n):
        far, far_p = far_y * 2 + xl, far_y * 2 + (1 - xl)
        source, part = (
            (partner, every),
            (down, every),
            (up, every),
            (down_p, every),
            (up_p, every),
            (far, low_half),
            (far, high_half),
            (far_p, low_half),
            (far_p, high_half),
        )[n]
        wait_bytes(kvg.at[h, source, part, :], r_a.at[h, n])

    def own(h):
        wait_bytes(kvg.at[h, me_dp], r_fin.at[h])
        for n in range(3):
            hop(h, n).start()
        out = pltpu.make_async_copy(kvg.at[h, me_dp], (dk_out, dv_out)[h], o_sem.at[h])
        out.start()

    def relay(h, n, sends):
        arrived(h, n)
        for m in sends:
            hop(h, m).start()

    out_rows = share // (NB * NC)
    n_tok = n_dp * tok

    def outgoing(h, n):
        return h_buf.at[:, n * out_rows : (n + 1) * out_rows, h * kv_cols : (h + 1) * kv_cols]

    def project(h):
        cols = slice(h * kv_cols, (h + 1) * kv_cols)
        grads = kvg[h].reshape(n_tok, kv_cols)
        step_rows = share // NZ
        for k in range(NZ):
            i = lax.rem(z + k, NZ)
            at = pl.ds(pl.multiple_of(i * step_rows, step_rows), step_rows)
            p_buf[at, cols] = dot(e_buf[at, 0:n_tok], grads)
            for xx in range(NX):
                b = i * NX + xx
                at = pl.ds(pl.multiple_of((b * NC + oc) * out_rows, out_rows), out_rows)
                outgoing(h, 0)[b] = p_buf[at, cols].astype(BF16)
            w_core(h, i).start()

    def w_core(h, i):
        some = pl.ds(i * NX, NX)
        dst = wc_recv.at[h, some]
        return remote(outgoing(h, 0).at[some], dst, s_wc.at[h, i], r_wc.at[h, i], ctx_dev(z, x, oc))

    def partial_sum(h, b):
        at = pl.ds(pl.multiple_of((b * NC + c) * out_rows, out_rows), out_rows)
        return p_buf[at, h * kv_cols : (h + 1) * kv_cols] + wc_recv[h, b].astype(F32)

    def spread(h):
        for k in range(NZ):
            i = lax.rem(z + k, NZ)
            w_core(h, i).wait_recv()
            for xx in range(NX):
                gx = lax.rem(x + xx, NX)
                b = i * NX + gx
                if k > 0 or xx > 0:
                    outgoing(h, 1)[b] = partial_sum(h, b).astype(BF16)
                    dst = w_recv.at[h, my_block]
                    remote(outgoing(h, 1).at[b], dst, s_w.at[h], r_w.at[h, my_block], ctx_dev(i, gx, c)).start()

    def collect(h):
        total = partial_sum(h, my_block)
        for d in range(1, NB):
            b = lax.rem(my_block + d, NB)
            wait_bytes(w_recv.at[h, b], r_w.at[h, b])
            total = total + w_recv[h, b].astype(F32)
        w_res[h] = total
        pltpu.make_async_copy(w_res.at[h], (wk_out, wv_out)[h], o_sem.at[2 + h]).start()

    own(0)
    relay(0, 0, (3,))
    own(1)
    relay(0, 1, (5,))
    relay(0, 2, (6, 4))
    relay(1, 0, (4,))
    relay(0, 3, (7,))
    relay(1, 1, (5, 3))
    relay(1, 2, (6,))
    relay(0, 4, (8,))
    for n in range(5, 9):
        arrived(0, n)
    project(0)
    relay(1, 3, (7,))
    relay(1, 4, (8,))
    spread(0)
    for n in range(5, 9):
        arrived(1, n)
    project(1)
    spread(1)
    collect(0)
    collect(1)

    wait_bytes(dq_out, r_dq)
    part = heads - per_dev
    wait_bytes(q_in.at[:, : part * HD], s_q)
    wait_bytes(g_in.at[:, : part * HD], s_g)
    wait_bytes(q_in.at[:, : part * HD], s_dq)
    wait_bytes(q_in.at[:, : (NB - 1) * 2 * HD], s_kv)
    for b in range(NB):
        wait_bytes(kv_buf.at[b, c], s_fw.at[b])
    wait_bytes(h_in.at[:, : (n_dp - 1) * share], s_h)
    for zz in range(NZ):
        over_core(zz).wait_send()
        over_x(zz).wait_send()
    wait_bytes(fin.at[pl.ds(0, NZ - 1)], s_fin)
    for h in range(2):
        for n in range(9):
            hop(h, n).wait_send()
        for i in range(NZ):
            w_core(h, i).wait_send()
        wait_bytes(w_recv.at[h, pl.ds(0, NB - 1)], s_w.at[h])
        wait_bytes(kvg.at[h, me_dp], o_sem.at[h])
        wait_bytes(w_res.at[h], o_sem.at[2 + h])


def copy_out(*refs):
    sources, targets, held, in_sem, out_sem = refs[:5], refs[5:10], refs[10:15], refs[15], refs[16]
    pieces = []
    for n in range(5):
        steps = 4 if n == 0 else 1
        size = sources[n].shape[0] // steps
        for i in range(steps):
            pieces.append((n, pl.ds(i * size, size)))
    ins = [pltpu.make_async_copy(sources[n].at[at], held[n].at[at], in_sem.at[k]) for k, (n, at) in enumerate(pieces)]
    outs = [pltpu.make_async_copy(held[n].at[at], targets[n].at[at], out_sem.at[k]) for k, (n, at) in enumerate(pieces)]
    for copy in ins:
        copy.start()
    for first, second in zip(ins, outs):
        first.wait()
        second.start()
    for copy in outs:
        copy.wait()


def on_device(n_dp, queries, keys, values, out_grad, hidden):
    tok, width = queries.shape
    kv_cols = keys.shape[1]
    blk = tok * NC
    per_dev = width // HD // (NZ * NC)
    rows = per_dev * blk
    share = hidden.shape[1] // n_dp
    out_rows = share // (NZ * NX * NC)
    dma = pltpu.SemaphoreType.DMA
    any_spec = pl.BlockSpec(memory_space=pl.ANY)
    assert n_dp * tok <= rows and share <= NB * blk and 2 * kv_cols <= rows and n_dp == NB == 8
    shapes = [
        jax.ShapeDtypeStruct(queries.shape, BF16),
        jax.ShapeDtypeStruct(keys.shape, BF16),
        jax.ShapeDtypeStruct(values.shape, BF16),
        jax.ShapeDtypeStruct((out_rows, kv_cols), F32),
        jax.ShapeDtypeStruct((out_rows, kv_cols), F32),
    ]
    results = pl.pallas_call(
        functools.partial(kernel, n_dp),
        out_shape=shapes,
        in_specs=[any_spec] * 5,
        out_specs=[any_spec] * 5,
        scratch_shapes=[
            pltpu.VMEM((NZ, per_dev, blk, HD), BF16),
            pltpu.VMEM((NZ, per_dev, blk, HD), BF16),
            pltpu.VMEM((NB, NC, 2, tok, HD), BF16),
            pltpu.VMEM((HD, rows), BF16),
            pltpu.VMEM((HD, rows), BF16),
            pltpu.VMEM((NB * blk, rows), BF16),
            pltpu.VMEM((NB * blk, rows), F32),
            pltpu.VMEM((NB, rows), F32),
            pltpu.VMEM((2, NB, NC, tok, HD), F32),
            pltpu.VMEM((HD, rows), F32),
            pltpu.VMEM((NB, 2, tok, HD), BF16),
            pltpu.VMEM((NB, 2, tok, HD), BF16),
            pltpu.VMEM((NZ, 2, tok, HD), BF16),
            pltpu.VMEM((NZ, 2, tok, HD), BF16),
            pltpu.VMEM((NZ, 2, tok, HD), BF16),
            pltpu.VMEM((n_dp, tok, share), BF16),
            pltpu.VMEM((2, n_dp, tok, kv_cols), BF16),
            pltpu.VMEM((2, NB, out_rows, kv_cols), BF16),
            pltpu.VMEM((2, NB, out_rows, kv_cols), BF16),
            pltpu.VMEM((2, out_rows, kv_cols), F32),
            dma,
            dma,
            dma,
            dma((NB,)),
            dma,
            dma,
            dma((NZ,)),
            dma((NZ,)),
            dma,
            dma((2, 9)),
            dma((2, NZ)),
            dma((2,)),
            dma((NZ,)),
            dma((NZ,)),
            dma((NB,)),
            dma((NB,)),
            dma,
            dma,
            dma((NZ,)),
            dma((NZ,)),
            dma((2,)),
            dma((2, 9)),
            dma((2, NZ)),
            dma((2, NB)),
            dma((4,)),
        ],
        compiler_params=pltpu.CompilerParams(
            collective_id=0, has_side_effects=True, vmem_limit_bytes=63 * 1024 * 1024
        ),
        cost_estimate=pl.CostEstimate(
            flops=40_000_000_000, bytes_accessed=20_000_000, transcendentals=10_000_000
        ),
        name="attention_backward",
    )(queries, keys, values, out_grad, hidden)
    return pl.pallas_call(
        copy_out,
        out_shape=shapes,
        in_specs=[any_spec] * 5,
        out_specs=[any_spec] * 5,
        scratch_shapes=[pltpu.VMEM(a.shape, a.dtype) for a in shapes] + [dma((8,)), dma((8,))],
        cost_estimate=pl.CostEstimate(flops=0, bytes_accessed=4_500_000, transcendentals=0),
        name="copy_out",
    )(*results)


def solution(mesh):
    spec = P(("dp", "ctx"), None)
    return jax.shard_map(
        functools.partial(on_device, mesh.shape["dp"]),
        mesh=mesh,
        in_specs=(spec,) * 5,
        out_specs=(spec,) * 5,
        check_vma=False,
    )
```
